512 devices in a mesh: space: 128 (over z, x, core), feat: 4 (over y).
Axes of the slice: x: 4, y: 4, z: 16, core: 2. Of those that a mesh axis runs over, the one named last changes fastest.
Arguments:
- bond_state: bfloat16 [262144, 512], P('space', 'feat'), may hold values from -6 to 6
- block_fill: int32 [2048], P('space'), may hold values from 64 to 128
- w_in: bfloat16 [512, 512], P(None, 'feat'), may hold values from -0.25 to 0.25
- w_down: bfloat16 [512, 64], P('feat'), may hold values from -0.25 to 0.25
- pair_coef: bfloat16 [14336, 128, 128], P('space'), may hold values from -0.5 to 0.5
- pair_source: int32 [14336], P('space'), may hold values from 0 to 15
- pair_owner: int32 [14336, 1], P('space'), may hold values from 0 to 127; in each aligned block of 112 rows (0 to 111, 112 to 223, ...) at most 2 rows name the same one
- pair_target: int32 [14336], P('space'), may hold values from 0 to 15
- w_gate: bfloat16 [64, 512], P(None, 'feat'), may hold values from -0.75 to 0.75
- w_atom_in: bfloat16 [64, 256], P(None, 'feat'), may hold values from -0.75 to 0.75
- atom_state: bfloat16 [256, 65536], P('feat', 'space'), may hold values from -6 to 6
- w_atom: bfloat16 [256, 256], P('feat'), may hold values from -0.375 to 0.375
- bond_ends: int32 [2, 262144], P(None, 'space'), may hold values from 0 to 1535
- w_left: bfloat16 [256, 512], P(None, 'feat'), may hold values from -0.375 to 0.375
- w_right: bfloat16 [256, 512], P(None, 'feat'), may hold values from -0.375 to 0.375
Outputs:
- bond_out: bfloat16 [262144, 512], P('space', 'feat')
- atom_out: bfloat16 [256, 65536], P('feat', 'space')
The draws below stay inside these ranges and needn't reach their ends.
Inputs may be any that keep to these rules, and one draw needn't show every extreme that they name: `pair_owner`: among the 112 pairs of one domain, at most 2 name the same owner, a bound that some block reaches.
All inputs are finite; a program needn't handle non-finite values.
Results may differ from the reference program's by a relative error of at most 0.008.
Values may be sent and summed in bfloat16 or wider, within the bound.
No kernel may reach another device: no remote copies, remote signals or barrier semaphores. Data moves between devices by JAX's collectives and lax.ppermute only.
A program may use at most 64 MiB of HBM per device.

```python
import math
import jax
import jax.numpy as jnp
import numpy as np
from jax import lax

DB = 512
DC = 64
DA = 256
BS = 128
BLK_DEV = 16
ATOM_DEV = 512
PAIR_DEV = 112
CAP = 2
NBLK = 2048
NBONDS = 262144
NATOMS = 65536
NPAIRS = 14336
N_SPACE = 128


def draw_bond_ends(key, part):
    first_key = jax.random.fold_in(key, 11)
    second_key = jax.random.fold_in(key, 23)
    region = jax.random.randint(first_key, (2, NBONDS), 0, 8)
    side = jnp.where(region == 0, 0, jnp.where(region == 7, 2, 1))
    within = jax.random.randint(second_key, (2, NBONDS), 0, ATOM_DEV)
    return (side * ATOM_DEV + within).astype(jnp.int32)


def place_ends(result, key, least, high):
    longest = result.shape.index(max(result.shape))
    spots = []
    for shift in (0, 1):
        where = [jax.random.randint(jax.random.fold_in(key, axis), (), 0, length) for axis, length in enumerate(result.shape)]
        where[longest] = (where[longest] + shift) % result.shape[longest]
        spots.append(tuple(where))
    return result.at[spots[0]].set(least).at[spots[1]].set(high)


def shard_levels(key, shape, pieces, smallest, high):
    factor_of = 1.0
    for dim, blocks in pieces:
        draws = jax.random.uniform(jax.random.fold_in(jax.random.fold_in(key, 6), dim), (blocks,), jnp.float32, smallest / len(pieces), high / len(pieces))
        factor_of = factor_of * jnp.repeat(jnp.exp(draws), shape[dim] // blocks).reshape((-1,) + (1,) * (len(shape) - 1 - dim))
    return factor_of


def shared_out(key, own, number, rows, amount, top, most, slope):
    sequence = jax.random.permutation(key, amount)
    packed, common = shares(amount, rows * top, most, slope, True), shares(amount, rows * top, most, slope, False)
    places = jnp.arange(amount)

    def named(tallies, turn):
        used = int((tallies > 0).sum())
        fixed = max(1, used // 4)
        shifted = fixed + (places - fixed + turn * (used - fixed)) % max(1, amount - fixed)
        return jnp.zeros((amount,), jnp.int32).at[sequence[jnp.where(places < fixed, places, shifted)]].set(jnp.asarray(tallies, jnp.int32))

    tallies = jnp.where(number % 4 == 0, named(packed, number // 4), named(common, number - number // 4 - 1))
    mixed = jax.random.permutation(jax.random.fold_in(own, 3), amount)
    giver, taker = mixed[0:amount // 2 * 2:2], mixed[1:amount // 2 * 2:2]
    margin = jnp.minimum(tallies[giver] - 1, most - tallies[taker]) // 2
    margin = jnp.where((giver == sequence[0]) | (taker == sequence[0]) | (tallies[taker] == 0), 0, jnp.maximum(margin, 0))
    shifted = jax.random.randint(jax.random.fold_in(own, 4), (amount // 2,), 0, 1 << 20) % (margin + 1)
    tallies = tallies.at[giver].add(-shifted).at[taker].add(shifted)
    labels = jnp.searchsorted(jnp.cumsum(tallies), jnp.arange(rows * top), side="right").astype(jnp.int32)
    table = labels.reshape(top, rows).T
    table = table[jax.random.permutation(jax.random.fold_in(own, 1), rows)]
    turn = jax.random.randint(jax.random.fold_in(own, 2), (rows, 1), 0, top)
    return jnp.take_along_axis(table, (jnp.arange(top)[None, :] + turn) % top, axis=1)


def shares(number_of, total, most, skew, full):
    loads = [(1 << 20) // math.isqrt(rank ** skew) + 1 for rank in range(1, number_of + 1)]
    largest = most if full else min(most, max(-(-total // number_of), total * loads[0] // sum(loads)))
    least = 1 if total - largest >= number_of - 1 else 0
    counts, rest = [largest] + [least] * (number_of - 1), total - largest - least * (number_of - 1)
    while rest > 0:
        candidates = [i for i in range(1, number_of) if counts[i] < largest] or [i for i in range(1, number_of) if counts[i] < most]
        pool, left = sum([loads[i] for i in candidates]), rest
        for i in candidates:
            extra = min(most - counts[i], max(1, left * loads[i] // pool), rest)
            counts[i] = counts[i] + extra
            rest = rest - extra
    return np.array(counts)


def centred(key, extent, width, most, shards=(), kind=jnp.bfloat16):
    result = width * jax.random.normal(key, extent, jnp.float32)
    if shards:
        result = result * shard_levels(key, extent, shards, -0.22, 0.18)
    return jnp.clip(result, -most, most).astype(kind)


def setup_inputs(seed: int = 0) -> dict:
    streams_of = jax.random.split(jax.random.key(seed), 16)
    bond_state = centred(streams_of[0], (NBONDS, DB), 1.0, 6.0, ((0, 128), (1, 4)))
    block_fill = place_ends(jax.random.randint(streams_of[1], (NBLK,), BS // 2, BS + 1), jax.random.fold_in(streams_of[1], 1), BS // 2, BS).astype(jnp.int32)
    w_in = centred(streams_of[2], (DB, DB), DB ** -0.5, 0.25, ((1, 4),))
    w_down = centred(streams_of[3], (DB, DC), DB ** -0.5, 0.25, ((0, 4),))
    pair_coef = centred(streams_of[4], (NPAIRS, BS, BS), BS ** -0.5, 0.5, ((0, 128),))
    pair_source = place_ends(jax.random.randint(streams_of[5], (NPAIRS,), 0, BLK_DEV), jax.random.fold_in(streams_of[5], 1), 0, BLK_DEV - 1).astype(jnp.int32)
    pair_owner_keys = jax.random.split(jax.random.fold_in(streams_of[6], 1), NPAIRS // PAIR_DEV)
    pair_owner_turns = jax.random.permutation(jax.random.fold_in(streams_of[6], 3), NPAIRS // PAIR_DEV)
    pair_owner = jax.vmap(lambda own, number: shared_out(jax.random.fold_in(streams_of[6], 2), own, number, PAIR_DEV, N_SPACE, 1, CAP, 2))(pair_owner_keys, pair_owner_turns).reshape((NPAIRS, 1))
    pair_target = place_ends(jax.random.randint(streams_of[7], (NPAIRS,), 0, BLK_DEV), jax.random.fold_in(streams_of[7], 1), 0, BLK_DEV - 1).astype(jnp.int32)
    w_gate = centred(streams_of[8], (DC, DB), DC ** -0.5, 0.75, ((1, 4),))
    w_atom_in = centred(streams_of[9], (DC, DA), DC ** -0.5, 0.75, ((1, 4),))
    atom_state = centred(streams_of[10], (DA, NATOMS), 1.0, 6.0, ((0, 4), (1, 128)))
    w_atom = centred(streams_of[11], (DA, DA), DA ** -0.5, 0.375, ((0, 4),))
    bond_ends = draw_bond_ends(jax.random.fold_in(streams_of[15], 71), 0)
    w_left = centred(streams_of[13], (DA, DB), DA ** -0.5, 0.375, ((1, 4),))
    w_right = centred(streams_of[14], (DA, DB), DA ** -0.5, 0.375, ((1, 4),))
    return dict(bond_state=bond_state, block_fill=block_fill, w_in=w_in, w_down=w_down, pair_coef=pair_coef, pair_source=pair_source, pair_owner=pair_owner, pair_target=pair_target, w_gate=w_gate, w_atom_in=w_atom_in, atom_state=atom_state, w_atom=w_atom, bond_ends=bond_ends, w_left=w_left, w_right=w_right)


def reference(bond_state, block_fill, w_in, w_down, pair_coef, pair_source, pair_owner, pair_target, w_gate, w_atom_in, atom_state, w_atom, bond_ends, w_left, w_right):
    bond_count = bond_state.shape[0]
    block_count = block_fill.shape[0]
    atom_count = atom_state.shape[1]
    position = jnp.arange(BS, dtype=jnp.int32)[None, :]
    real_mask = (position < block_fill[:, None]).astype(jnp.float32).reshape(bond_count)
    hidden = jax.nn.silu(jnp.dot(bond_state, w_in, preferred_element_type=jnp.float32)).astype(jnp.bfloat16)
    angular = (jnp.dot(hidden, w_down, preferred_element_type=jnp.float32) * real_mask[:, None]).astype(jnp.bfloat16)
    angular_blocks = angular.reshape(block_count, BS, DC)
    pair_device = jnp.arange(NPAIRS, dtype=jnp.int32) // PAIR_DEV
    source_ids = (pair_device * BLK_DEV + pair_source).astype(jnp.int32)
    target_ids = (pair_owner[:, 0] * BLK_DEV + pair_target).astype(jnp.int32)

    def one_device(running, device):
        first_pair = (device * PAIR_DEV).astype(jnp.int32)
        own_sources = lax.dynamic_slice_in_dim(source_ids, first_pair, PAIR_DEV)
        own_targets = lax.dynamic_slice_in_dim(target_ids, first_pair, PAIR_DEV)
        coefficients = lax.dynamic_slice_in_dim(pair_coef, first_pair, PAIR_DEV, 0).astype(jnp.float32)
        gathered = angular_blocks[own_sources].astype(jnp.float32)
        contrib = jnp.einsum("pij,pjc->pic", coefficients, gathered)
        rounded = lax.optimization_barrier(contrib.astype(jnp.bfloat16)).astype(jnp.float32)
        return running.at[own_targets].add(rounded), None

    start_sum = jnp.zeros((block_count, BS, DC), jnp.float32)
    block_sums, unused = lax.scan(one_device, start_sum, jnp.arange(N_SPACE, dtype=jnp.int32))
    message = (block_sums.reshape(bond_count, DC) * real_mask[:, None]).astype(jnp.bfloat16)
    gate_pre = jnp.dot(message, w_gate, preferred_element_type=jnp.float32)
    to_atoms = jnp.dot(message, w_atom_in, preferred_element_type=jnp.float32)
    bond_device = jnp.arange(bond_count, dtype=jnp.int32) // (BLK_DEV * BS)
    window_base = bond_device * ATOM_DEV - ATOM_DEV
    left_atoms = ((window_base + bond_ends[0]) % atom_count).astype(jnp.int32)
    right_atoms = ((window_base + bond_ends[1]) % atom_count).astype(jnp.int32)
    atom_sums = jax.ops.segment_sum(to_atoms, right_atoms, num_segments=atom_count)
    atom_counts = jax.ops.segment_sum(real_mask, right_atoms, num_segments=atom_count)
    mean_in = (atom_sums / jnp.maximum(atom_counts, 1.0)[:, None]).astype(jnp.bfloat16)
    atom_pre = jnp.dot(mean_in, w_atom, preferred_element_type=jnp.float32)
    atom_new = (atom_state.T.astype(jnp.float32) + jax.nn.silu(atom_pre)).astype(jnp.bfloat16)
    mixed_atoms = jnp.dot(atom_new[left_atoms], w_left, preferred_element_type=jnp.float32) + jnp.dot(atom_new[right_atoms], w_right, preferred_element_type=jnp.float32)
    update = jax.nn.sigmoid(gate_pre) * (hidden.astype(jnp.float32) + jax.nn.silu(mixed_atoms))
    bond_out = (bond_state.astype(jnp.float32) + real_mask[:, None] * update).astype(jnp.bfloat16)
    return bond_out, atom_new.T
```

```python
import functools

import jax
import jax.numpy as jnp
from jax import lax
from jax.experimental import pallas as pl
from jax.experimental.pallas import tpu as pltpu
from jax.sharding import PartitionSpec as P

BF16 = jnp.bfloat16
F32 = jnp.float32
BLOCK = 128
LANES = 128
SLOTS = 2
SPAN = 4
HALO = 3
LEFT_FIRST = (((0,), (0,)), ((), ()))
BOTH_LAST = (((1,), (1,)), ((), ()))


def vmem():
    return pl.BlockSpec(memory_space=pltpu.VMEM)


def smem():
    return pl.BlockSpec(memory_space=pltpu.SMEM)


def dot(a, b, dims):
    return lax.dot_general(a, b, dims, preferred_element_type=F32)


def exchanged(value, axis, groups=None):
    return lax.all_to_all(
        value, axis, split_axis=0, concat_axis=0, tiled=True, axis_index_groups=groups
    )


def for_each(value, axis):
    return jnp.broadcast_to(value, (lax.axis_size(axis), *value.shape))


def angular_body(fill_ref, place_ref, x_ref, w_ref, down_ref, hidden_ref, angular_ref):
    quarters = x_ref.shape[0]
    own_blocks = angular_ref.shape[1]
    channels = angular_ref.shape[2]
    first = place_ref[0] * own_blocks
    x = jnp.concatenate([x_ref[k] for k in range(quarters)], axis=1)
    total = None
    for q in range(quarters):
        pre = jnp.dot(x, w_ref[q], preferred_element_type=F32)
        hidden = jax.nn.silu(pre).astype(BF16)
        hidden_ref[q] = hidden
        part = dot(down_ref[q], hidden, BOTH_LAST)
        total = part if total is None else total + part
    for b in range(own_blocks):
        piece = total[:, b * BLOCK : (b + 1) * BLOCK]
        real = lax.broadcasted_iota(jnp.int32, piece.shape, 1) < fill_ref[first + b]
        piece = jnp.where(real, piece, 0.0).astype(BF16)
        for q in range(quarters):
            angular_ref[q, b] = piece[q * channels : (q + 1) * channels]


def angular_call(fill, place, x, w, down, own_blocks):
    quarters, bonds, width = x.shape
    channels = down.shape[1] // quarters
    return pl.pallas_call(
        angular_body,
        out_shape=(
            jax.ShapeDtypeStruct((quarters, bonds, w.shape[2]), BF16),
            jax.ShapeDtypeStruct((quarters, own_blocks, channels, BLOCK), BF16),
        ),
        in_specs=[smem(), smem(), vmem(), vmem(), vmem()],
        out_specs=(vmem(), vmem()),
        cost_estimate=pl.CostEstimate(
            flops=600_000_000, bytes_accessed=2_000_000, transcendentals=262_144
        ),
        name="angular",
    )(fill, place, x, w, down)


def contribution_body(chunk, source_ref, slot_ref, angular_ref, coef_ref, out_ref):
    step = pl.program_id(0)

    @pl.when(step == 0)
    def _():
        out_ref[...] = jnp.zeros_like(out_ref)

    for k in range(chunk):
        pair = step * chunk + k
        part = dot(angular_ref[source_ref[pair]], coef_ref[k], BOTH_LAST)
        out_ref[slot_ref[pair]] = part.astype(BF16)


def contribution_call(sources, slots, angular, coef, slot_count):
    pairs = coef.shape[0]
    chunk = next(c for c in (16, 14, 8, 7, 4, 2, 1) if pairs % c == 0)
    blocks, channels, rows = angular.shape
    return pl.pallas_call(
        functools.partial(contribution_body, chunk),
        out_shape=jax.ShapeDtypeStruct((slot_count, channels, rows), BF16),
        grid=(pairs // chunk,),
        in_specs=[
            smem(),
            smem(),
            pl.BlockSpec(angular.shape, lambda i: (0, 0, 0)),
            pl.BlockSpec((chunk, *coef.shape[1:]), lambda i: (i, 0, 0)),
        ],
        out_specs=pl.BlockSpec((slot_count, channels, rows), lambda i: (0, 0, 0)),
        cost_estimate=pl.CostEstimate(
            flops=60_000_000, bytes_accessed=5_000_000, transcendentals=0
        ),
        name="contribution",
    )(sources, slots, angular, coef)


def message_body(
    label_ref,
    fill_ref,
    place_ref,
    ends_ref,
    arrived_ref,
    message_ref,
    own_ref,
    near_ref,
    far_ref,
    sums,
    padded,
):
    blocks = fill_ref.shape[0]
    slots, channels, rows = arrived_ref.shape
    bonds = blocks * rows
    spans = HALO * SPAN
    sums[...] = jnp.zeros_like(sums)

    def add(step, carry):
        for k in range(8):
            slot = step * 8 + k
            label = label_ref[slot]
            sums[label] += arrived_ref[slot].astype(F32)
        return carry

    lax.fori_loop(0, slots // 8, add, 0)
    pieces = []
    masks = []
    for b in range(blocks):
        real = lax.broadcasted_iota(jnp.int32, (channels, rows), 1) < fill_ref[b]
        piece = jnp.where(real, sums[b], 0.0)
        message_ref[:, b * rows : (b + 1) * rows] = piece.astype(BF16)
        pieces.append(piece)
        masks.append(jnp.where(real[:1], 1.0, 0.0))
    message = jnp.concatenate(pieces, axis=1)
    mask = jnp.concatenate(masks, axis=1)
    ends = ends_ref[1:2, :]
    high = ends // LANES
    low = ends % LANES
    stacked = []
    tallies = []
    for h in range(spans):
        here = high == h
        stacked.append(jnp.where(here, message, 0.0).astype(BF16))
        tallies.append(jnp.where(here, mask, 0.0))
    tallies.append(jnp.zeros((16 - spans, bonds), F32))
    stacked.append(jnp.concatenate(tallies, axis=0).astype(BF16))
    chosen = jnp.where(
        low == lax.broadcasted_iota(jnp.int32, (LANES, bonds), 0), 1.0, 0.0
    ).astype(BF16)
    window = dot(jnp.concatenate(stacked, axis=0), chosen, BOTH_LAST)
    counts = window[spans * channels : spans * channels + spans]
    upper = jnp.floor(counts * (1.0 / 256.0))
    lower = counts - 256.0 * upper
    padded[...] = jnp.zeros_like(padded)
    width = SPAN * channels
    for k in range(HALO):
        group = jnp.concatenate(
            [
                window[k * width : (k + 1) * width],
                upper[k * SPAN : (k + 1) * SPAN],
                lower[k * SPAN : (k + 1) * SPAN],
            ],
            axis=0,
        )
        own_ref[k] = group
        padded[HALO + k] = group.astype(BF16)
    domain = place_ref[0]
    near = domain % 4
    far = (domain + 2) % 4
    for m in range(4):
        start = jnp.where(m == near, 0, m - near + HALO)
        across = (m < 2) != (far < 2)
        start_far = jnp.where(across, m - far + HALO, 0)
        for k in range(HALO):
            near_ref[m, k] = padded[start + k]
            far_ref[m, k] = padded[start_far + k]


def message_call(labels, fill, place, ends, arrived):
    slots, channels, rows = arrived.shape
    blocks = fill.shape[0]
    depth = SPAN * channels + 2 * SPAN
    return pl.pallas_call(
        message_body,
        out_shape=(
            jax.ShapeDtypeStruct((channels, blocks * rows), BF16),
            jax.ShapeDtypeStruct((HALO, depth, LANES), F32),
            jax.ShapeDtypeStruct((4, HALO, depth, LANES), BF16),
            jax.ShapeDtypeStruct((4, HALO, depth, LANES), BF16),
        ),
        in_specs=[smem(), smem(), smem(), vmem(), vmem()],
        out_specs=(vmem(), vmem(), vmem(), vmem()),
        scratch_shapes=[
            pltpu.VMEM((blocks + 1, channels, rows), F32),
            pltpu.VMEM((3 * HALO, depth, LANES), BF16),
        ],
        cost_estimate=pl.CostEstimate(
            flops=120_000_000, bytes_accessed=2_000_000, transcendentals=0
        ),
        name="message",
    )(labels, fill, place, ends, arrived)


def mean_body(own_ref, near_ref, far_ref, out_ref):
    copies = out_ref.shape[0]
    depth = own_ref.shape[1]
    channels = (depth - 2 * SPAN) // SPAN
    width = SPAN * channels
    for k in range(HALO):
        total = own_ref[k]
        for m in range(4):
            total += near_ref[m, k].astype(F32) + far_ref[m, k].astype(F32)
        for h in range(SPAN):
            count = 256.0 * total[width + h : width + h + 1]
            count += total[width + SPAN + h : width + SPAN + h + 1]
            mean = total[h * channels : (h + 1) * channels] / jnp.maximum(count, 1.0)
            mean = mean.astype(BF16)
            row = (k * SPAN + h) * channels
            for m in range(copies):
                out_ref[m, row : row + channels] = mean


def mean_call(own, near, far, copies):
    channels = (own.shape[1] - 2 * SPAN) // SPAN
    return pl.pallas_call(
        mean_body,
        out_shape=jax.ShapeDtypeStruct((copies, HALO * SPAN * channels, LANES), BF16),
        in_specs=[vmem()] * 3,
        out_specs=vmem(),
        cost_estimate=pl.CostEstimate(
            flops=1_000_000, bytes_accessed=600_000, transcendentals=0
        ),
        name="mean",
    )(own, near, far)


def update_body(
    fill_ref,
    place_ref,
    mean_ref,
    atoms_ref,
    left_ref,
    right_ref,
    gate_ref,
    message_ref,
    hidden_ref,
    bonds_ref,
    ends_ref,
    bond_out_ref,
    atom_out_ref,
    table_left,
    table_right,
    kept,
):
    quarters = mean_ref.shape[0]
    channels = message_ref.shape[1]
    features = atoms_ref.shape[1]
    window = HALO * SPAN * LANES
    inputs = quarters * features
    tile = 2 * LANES
    atom_dim = window
    states = jnp.concatenate(
        [atoms_ref[f, :, window : window + inputs] for f in range(quarters)], axis=0
    )
    sides = jnp.concatenate([left_ref[...], right_ref[...]], axis=1)
    width = left_ref.shape[1]
    own_start = window // HALO
    for c in range(window // tile):
        columns = slice(c * tile, (c + 1) * tile)
        mean = jnp.concatenate(
            [
                jnp.concatenate(
                    [
                        mean_ref[f, (2 * c + e) * channels : (2 * c + e + 1) * channels]
                        for f in range(quarters)
                    ],
                    axis=0,
                )
                for e in range(2)
            ],
            axis=1,
        )
        mean_in = jnp.concatenate(
            [
                dot(
                    atoms_ref[f, :, window + inputs : window + inputs + features],
                    mean,
                    LEFT_FIRST,
                ).astype(BF16)
                for f in range(quarters)
            ],
            axis=0,
        )
        pre = dot(states, mean_in, LEFT_FIRST)
        state = jnp.concatenate([atoms_ref[f, :, columns] for f in range(quarters)], axis=0)
        updated = (state.astype(F32) + jax.nn.silu(pre)).astype(BF16)
        place = c * tile - own_start
        if 0 <= place < own_start:
            kept[:, place : place + tile] = updated
        table = dot(updated, sides, LEFT_FIRST).astype(BF16)
        table_left[:, c * width : (c + 1) * width] = table[:, :width]
        table_right[:, c * width : (c + 1) * width] = table[:, width:]
    own = pl.multiple_of(place_ref[0] * features, features)
    atom_out_ref[...] = kept[pl.ds(own, features), :]
    bonds = bonds_ref.shape[0]
    per_quarter = bonds // quarters
    lane = lax.broadcasted_iota(jnp.int32, (tile, tile), 1)
    row = lax.broadcasted_iota(jnp.int32, (BLOCK, width), 0)
    for t in range(bonds // tile):
        rows = slice(t * tile, (t + 1) * tile)
        mixed = None
        for side, table in ((0, table_left), (1, table_right)):
            end = ends_ref[rows, side : side + 1]
            chosen = jnp.where(end % tile == lane, 1.0, 0.0).astype(BF16)
            found = jnp.dot(chosen, table[...], preferred_element_type=F32)
            high = jnp.broadcast_to(end // tile, (tile, width))
            for c in range(window // tile):
                part = jnp.where(high == c, found[:, c * width : (c + 1) * width], 0.0)
                mixed = part if mixed is None else mixed + part
        message = jnp.concatenate([message_ref[f, :, rows] for f in range(quarters)], axis=0)
        gate = dot(message, gate_ref[...], LEFT_FIRST)
        q = t * tile // per_quarter
        start = t * tile - q * per_quarter
        hidden = hidden_ref[q, start : start + tile].astype(F32)
        update = jax.nn.sigmoid(gate) * (hidden + jax.nn.silu(mixed))
        for e in range(tile // BLOCK):
            part = slice(e * BLOCK, (e + 1) * BLOCK)
            real = row < fill_ref[t * (tile // BLOCK) + e]
            here = slice(t * tile + e * BLOCK, t * tile + (e + 1) * BLOCK)
            bond_out_ref[here] = (
                bonds_ref[here].astype(F32) + jnp.where(real, update[part], 0.0)
            ).astype(BF16)


def update_call(fill, place, mean, atoms, left, right, gate, message, hidden, bonds, ends):
    features = atoms.shape[1]
    window = HALO * SPAN * LANES
    width = left.shape[1]
    tile = 2 * LANES
    return pl.pallas_call(
        update_body,
        out_shape=(
            jax.ShapeDtypeStruct(bonds.shape, BF16),
            jax.ShapeDtypeStruct((features, window // HALO), BF16),
        ),
        in_specs=[smem(), smem()] + [vmem()] * 9,
        out_specs=(vmem(), vmem()),
        scratch_shapes=[
            pltpu.VMEM((tile, window // tile * width), BF16),
            pltpu.VMEM((tile, window // tile * width), BF16),
            pltpu.VMEM((mean.shape[0] * features, window // HALO), BF16),
        ],
        cost_estimate=pl.CostEstimate(
            flops=2_500_000_000, bytes_accessed=4_000_000, transcendentals=2_000_000
        ),
        name="update",
    )(fill, place, mean, atoms, left, right, gate, message, hidden, bonds, ends)


def local(
    bond_state,
    block_fill,
    w_in,
    w_down,
    pair_coef,
    pair_source,
    pair_owner,
    pair_target,
    w_gate,
    w_atom_in,
    atom_state,
    w_atom,
    bond_ends,
    w_left,
    w_right,
):
    spaces = lax.axis_size("space")
    feats = lax.axis_size("feat")
    space = lax.axis_index("space").astype(jnp.int32).reshape(1)
    feat = lax.axis_index("feat").astype(jnp.int32).reshape(1)
    bonds, width = bond_state.shape
    blocks = block_fill.shape[0]
    pairs = pair_source.shape[0]
    near_groups = [[4 * i + k for k in range(4)] for i in range(spaces // 4)]
    far_groups = [[(4 * i + 2 + k) % spaces for k in range(4)] for i in range(spaces // 4)]

    x = exchanged(bond_state.reshape(feats, bonds // feats, width), "feat")
    w = exchanged(for_each(w_in, "feat"), "feat")
    down = exchanged(for_each(w_down.T, "feat"), "feat")
    hidden, angular = angular_call(block_fill, feat, x, w, down, blocks // feats)
    angular = exchanged(angular, "feat")
    angular = angular.reshape(blocks, *angular.shape[2:])

    owners = pair_owner[:, 0]
    before = lax.broadcasted_iota(jnp.int32, (pairs, pairs), 1) < lax.broadcasted_iota(
        jnp.int32, (pairs, pairs), 0
    )
    rank = jnp.sum(jnp.where(before & (owners[:, None] == owners[None, :]), 1, 0), axis=1)
    slots = owners * SLOTS + rank
    wanted = slots[:, None] == lax.broadcasted_iota(jnp.int32, (pairs, spaces * SLOTS), 1)
    labels = blocks + jnp.sum(jnp.where(wanted, pair_target[:, None] - blocks, 0), axis=0)
    outgoing = contribution_call(pair_source, slots, angular, pair_coef, spaces * SLOTS)
    outgoing, labels, hidden = lax.optimization_barrier((outgoing, labels, hidden))
    arrived = exchanged(outgoing.reshape(spaces, SLOTS, *outgoing.shape[1:]), "space")
    arrived = arrived.reshape(outgoing.shape)
    hidden = exchanged(hidden, "feat")
    upward = [(i, (i + 1) % spaces) for i in range(spaces)]
    downward = [((i + 1) % spaces, i) for i in range(spaces)]
    atom_near, labels = lax.optimization_barrier((atom_state, labels))
    pack = jnp.concatenate(
        [
            lax.ppermute(atom_near, "space", upward),
            atom_near,
            lax.ppermute(atom_near, "space", downward),
            w_atom,
            w_atom_in,
        ],
        axis=1,
    )
    pack = exchanged(for_each(pack, "feat"), "feat")
    labels = exchanged(labels.reshape(spaces, SLOTS), "space").reshape(spaces * SLOTS)

    message, own, near, far = message_call(labels, block_fill, space, bond_ends, arrived)
    near = exchanged(near, "space", near_groups)
    far = exchanged(far, "space", far_groups)
    message = exchanged(for_each(message, "feat"), "feat")
    mean = exchanged(mean_call(own, near, far, feats), "feat")
    return update_call(
        block_fill,
        feat,
        mean,
        pack,
        w_left,
        w_right,
        w_gate,
        message,
        hidden,
        bond_state,
        bond_ends.T,
    )


def solution(mesh):
    placed = (
        P("space", "feat"),
        P("space"),
        P(None, "feat"),
        P("feat", None),
        P("space", None, None),
        P("space"),
        P("space", None),
        P("space"),
        P(None, "feat"),
        P(None, "feat"),
        P("feat", "space"),
        P("feat", None),
        P(None, "space"),
        P(None, "feat"),
        P(None, "feat"),
    )
    return jax.shard_map(
        local,
        mesh=mesh,
        in_specs=placed,
        out_specs=(P("space", "feat"), P("feat", "space")),
        check_vma=False,
    )
```

```python
import functools

import jax
import jax.numpy as jnp
from jax import lax
from jax.experimental import pallas as pl
from jax.experimental.pallas import tpu as pltpu
from jax.sharding import PartitionSpec as P


BF16 = jnp.bfloat16
F32 = jnp.float32
BLOCK = 128
LANES = 128
SLOTS = 2
SPAN = 4
HALO = 3
ROOM = 24 << 20
LEFT_FIRST = (((0,), (0,)), ((), ()))
BOTH_LAST = (((1,), (1,)), ((), ()))


def vmem():
    return pl.BlockSpec(memory_space=pltpu.VMEM)


def smem():
    return pl.BlockSpec(memory_space=pltpu.SMEM)


def dot(a, b, dims):
    return lax.dot_general(a, b, dims, preferred_element_type=F32)


def exchanged(value, axis, groups=None):
    return lax.all_to_all(
        value, axis, split_axis=0, concat_axis=0, tiled=True, axis_index_groups=groups
    )


def for_each(value, axis):
    return jnp.broadcast_to(value, (lax.axis_size(axis), *value.shape))


def moved(value, axis, steps):
    count = lax.axis_size(axis)
    return lax.ppermute(value, axis, [(i, (i + steps) % count) for i in range(count)])


def swapped(places, count, step):
    out = []
    for place in places:
        below = (place - step) % count
        out += [(place, below), (below, place)]
    return out


def angular_body(fill_ref, place_ref, pack_ref, hidden_ref, angular_ref):
    quarters, own_blocks, channels = angular_ref.shape[:3]
    bonds, width = hidden_ref.shape[1:]
    inputs = quarters * width
    feat = place_ref[0]
    first = feat * own_blocks
    x = jnp.concatenate([pack_ref[k, :bonds] for k in range(quarters)], axis=1)
    total = None
    for q in range(quarters):
        pre = jnp.dot(x, pack_ref[q, bonds : bonds + inputs], preferred_element_type=F32)
        hidden = jax.nn.silu(pre).astype(BF16)
        hidden_ref[(q - feat + quarters) % quarters] = hidden
        part = dot(pack_ref[q, bonds + inputs :], hidden, BOTH_LAST)
        total = part if total is None else total + part
    for b in range(own_blocks):
        piece = total[:, b * BLOCK : (b + 1) * BLOCK]
        real = lax.broadcasted_iota(jnp.int32, piece.shape, 1) < fill_ref[first + b]
        piece = jnp.where(real, piece, 0.0).astype(BF16)
        for q in range(quarters):
            angular_ref[q, b] = piece[q * channels : (q + 1) * channels]


def angular_call(fill, place, pack, bonds, own_blocks, channels):
    quarters, _, width = pack.shape
    return pl.pallas_call(
        angular_body,
        out_shape=(
            jax.ShapeDtypeStruct((quarters, bonds, width), BF16),
            jax.ShapeDtypeStruct((quarters, own_blocks, channels, BLOCK), BF16),
        ),
        in_specs=[smem(), smem(), vmem()],
        out_specs=(vmem(), vmem()),
        cost_estimate=pl.CostEstimate(
            flops=600_000_000, bytes_accessed=2_000_000, transcendentals=262_144
        ),
        compiler_params=pltpu.CompilerParams(vmem_limit_bytes=ROOM),
        name="angular",
    )(fill, place, pack)


def contribution_body(
    chunks, source_ref, slot_ref, label_ref, angular_ref, coef_hbm, out_ref, coef_ref, sems
):
    channels, rows = angular_ref.shape[1:]
    half = channels // 2
    stride = SLOTS * half + 1
    per_chunk = coef_ref.shape[0] // chunks
    copies = []
    for c in range(chunks):
        here = pl.ds(c * per_chunk, per_chunk)
        copies.append(pltpu.make_async_copy(coef_hbm.at[here], coef_ref.at[here], sems.at[c]))
        copies[c].start()
    out_ref[...] = jnp.zeros_like(out_ref)

    def tag(step, carry):
        for k in range(4):
            owner = step * 4 + k
            out_ref[owner * stride + stride - 1] = label_ref[owner]
        return carry

    lax.fori_loop(0, label_ref.shape[0] // 4, tag, 0)
    for c in range(chunks):
        copies[c].wait()

        def multiply(step, carry):
            for k in range(7):
                pair = c * per_chunk + step * 7 + k
                part = dot(angular_ref[source_ref[pair]], coef_ref[pair], BOTH_LAST)
                part = part.astype(BF16).reshape(half, 2, rows)
                out_ref[pl.ds(slot_ref[pair], half)] = part
            return carry

        lax.fori_loop(0, per_chunk // 7, multiply, 0)


def contribution_call(sources, slots, labels, angular, coef):
    pairs = coef.shape[0]
    chunks = next(c for c in (4, 2, 1) if pairs % (7 * c) == 0)
    _, channels, rows = angular.shape
    stride = SLOTS * channels // 2 + 1
    return pl.pallas_call(
        functools.partial(contribution_body, chunks),
        out_shape=jax.ShapeDtypeStruct((labels.shape[0] * stride, 2, rows), BF16),
        in_specs=[
            smem(),
            smem(),
            vmem(),
            vmem(),
            pl.BlockSpec(memory_space=pltpu.HBM),
        ],
        out_specs=vmem(),
        scratch_shapes=[
            pltpu.VMEM(coef.shape, BF16),
            pltpu.SemaphoreType.DMA((chunks,)),
        ],
        cost_estimate=pl.CostEstimate(
            flops=60_000_000, bytes_accessed=5_000_000, transcendentals=0
        ),
        compiler_params=pltpu.CompilerParams(vmem_limit_bytes=ROOM),
        name="contribution",
    )(sources, slots, labels, angular, coef)


def message_body(
    fill_ref,
    place_ref,
    ends_ref,
    arrived_ref,
    message_ref,
    own_ref,
    near_ref,
    next_ref,
    over_ref,
    sums,
    padded,
    labels,
    label_ref,
    sem,
):
    blocks = fill_ref.shape[0]
    channels, rows = sums.shape[1:]
    half = channels // 2
    stride = SLOTS * half + 1
    sources = arrived_ref.shape[0] // stride
    bonds = blocks * rows
    spans = HALO * SPAN
    total = jnp.zeros((2, rows), F32)
    for source in range(sources):
        total += arrived_ref[source * stride + stride - 1].astype(F32)
    labels[...] = total.astype(jnp.int32)
    copy = pltpu.make_async_copy(labels, label_ref, sem)
    copy.start()
    sums[...] = jnp.zeros_like(sums)
    copy.wait()

    def add(step, carry):
        for k in range(4):
            source = step * 4 + k
            for slot in range(SLOTS):
                part = arrived_ref[pl.ds(source * stride + slot * half, half)]
                sums[label_ref[slot, source]] += part.reshape(channels, rows).astype(F32)
        return carry

    lax.fori_loop(0, sources // 4, add, 0)
    pieces = []
    masks = []
    for b in range(blocks):
        real = lax.broadcasted_iota(jnp.int32, (channels, rows), 1) < fill_ref[b]
        piece = jnp.where(real, sums[b], 0.0)
        message_ref[b * channels : (b + 1) * channels] = piece.astype(BF16)
        pieces.append(piece)
        masks.append(jnp.where(real[:1], 1.0, 0.0))
    message = jnp.concatenate(pieces, axis=1)
    mask = jnp.concatenate(masks, axis=1)
    ends = ends_ref[1:2, :]
    high = ends // LANES
    low = ends % LANES
    stacked = []
    tallies = []
    for h in range(spans):
        here = high == h
        stacked.append(jnp.where(here, message, 0.0).astype(BF16))
        tallies.append(jnp.where(here, mask, 0.0))
    tallies.append(jnp.zeros((16 - spans, bonds), F32))
    stacked.append(jnp.concatenate(tallies, axis=0).astype(BF16))
    chosen = jnp.where(
        low == lax.broadcasted_iota(jnp.int32, (LANES, bonds), 0), 1.0, 0.0
    ).astype(BF16)
    window = dot(jnp.concatenate(stacked, axis=0), chosen, BOTH_LAST)
    counts = window[spans * channels : spans * channels + spans]
    upper = jnp.floor(counts * (1.0 / 256.0))
    lower = counts - 256.0 * upper
    padded[...] = jnp.zeros_like(padded)
    width = SPAN * channels
    for k in range(HALO):
        group = jnp.concatenate(
            [
                window[k * width : (k + 1) * width],
                upper[k * SPAN : (k + 1) * SPAN],
                lower[k * SPAN : (k + 1) * SPAN],
            ],
            axis=0,
        )
        own_ref[k] = group
        padded[HALO + k] = group.astype(BF16)
    near = place_ref[0] % 4
    for m in range(4):
        start = jnp.where(m == near, 0, m - near + HALO)
        for k in range(HALO):
            near_ref[m, k] = padded[start + k]
    first = HALO + jnp.where(near == 3, 1, 0)
    next_ref[0] = padded[first]
    next_ref[1] = padded[first + 1]
    over_ref[...] = padded[HALO + jnp.where(near >= 2, 2, 0)]


def message_call(fill, place, ends, arrived, channels):
    rows = arrived.shape[2]
    blocks = fill.shape[0]
    depth = SPAN * channels + 2 * SPAN
    return pl.pallas_call(
        message_body,
        out_shape=(
            jax.ShapeDtypeStruct((blocks * channels, rows), BF16),
            jax.ShapeDtypeStruct((HALO, depth, LANES), F32),
            jax.ShapeDtypeStruct((4, HALO, depth, LANES), BF16),
            jax.ShapeDtypeStruct((2, depth, LANES), BF16),
            jax.ShapeDtypeStruct((depth, LANES), BF16),
        ),
        in_specs=[smem(), smem(), vmem(), vmem()],
        out_specs=(vmem(), vmem(), vmem(), vmem(), vmem()),
        scratch_shapes=[
            pltpu.VMEM((blocks + 1, channels, rows), F32),
            pltpu.VMEM((3 * HALO, depth, LANES), BF16),
            pltpu.VMEM((SLOTS, LANES), jnp.int32),
            pltpu.SMEM((SLOTS, LANES), jnp.int32),
            pltpu.SemaphoreType.DMA(()),
        ],
        cost_estimate=pl.CostEstimate(
            flops=120_000_000, bytes_accessed=2_000_000, transcendentals=0
        ),
        compiler_params=pltpu.CompilerParams(vmem_limit_bytes=ROOM),
        name="message",
    )(fill, place, ends, arrived)


def mean_body(place_ref, own_ref, near_ref, next_ref, over_ref, message_ref, out_ref, total):
    copies = out_ref.shape[0]
    depth = own_ref.shape[1]
    channels = (depth - 2 * SPAN) // SPAN
    width = SPAN * channels
    spot = place_ref[0] % 4
    for k in range(HALO):
        value = own_ref[k]
        for m in range(4):
            value += near_ref[m, k].astype(F32)
        total[k] = value
    first = jnp.where(spot == 3, 1, 0)
    total[first] += next_ref[0].astype(F32)
    total[first + 1] += next_ref[1].astype(F32)
    total[jnp.where(spot >= 2, 2, 0)] += over_ref[...].astype(F32)
    for k in range(HALO):
        value = total[k]
        for h in range(SPAN):
            count = 256.0 * value[width + h : width + h + 1]
            count += value[width + SPAN + h : width + SPAN + h + 1]
            mean = value[h * channels : (h + 1) * channels] / jnp.maximum(count, 1.0)
            mean = mean.astype(BF16)
            row = (k * SPAN + h) * channels
            for m in range(copies):
                out_ref[m, row : row + channels] = mean
    for m in range(copies):
        out_ref[m, HALO * width :] = message_ref[...]


def mean_call(place, own, near, beside, over, message, copies):
    depth = own.shape[1]
    width = depth - 2 * SPAN
    rows = HALO * width + message.shape[0]
    return pl.pallas_call(
        mean_body,
        out_shape=jax.ShapeDtypeStruct((copies, rows, LANES), BF16),
        in_specs=[smem()] + [vmem()] * 5,
        out_specs=vmem(),
        scratch_shapes=[pltpu.VMEM((HALO, depth, LANES), F32)],
        cost_estimate=pl.CostEstimate(
            flops=1_000_000, bytes_accessed=600_000, transcendentals=0
        ),
        compiler_params=pltpu.CompilerParams(vmem_limit_bytes=ROOM),
        name="mean",
    )(place, own, near, beside, over, message)


def update_body(
    fill_ref,
    place_ref,
    mean_ref,
    atoms_ref,
    left_ref,
    right_ref,
    gate_ref,
    hidden_ref,
    bonds_ref,
    ends_ref,
    bond_out_ref,
    atom_out_ref,
    table_left,
    table_right,
    kept,
):
    quarters = mean_ref.shape[0]
    channels = gate_ref.shape[0] // quarters
    feat = place_ref[0]
    near = [(feat - q + quarters) % quarters for q in range(quarters)]
    after = HALO * SPAN * channels
    features = atoms_ref.shape[1]
    window = HALO * SPAN * LANES
    inputs = quarters * features
    tile = 2 * LANES
    states = jnp.concatenate(
        [atoms_ref[near[f], :, window : window + inputs] for f in range(quarters)], axis=0
    )
    sides = jnp.concatenate([left_ref[...], right_ref[...]], axis=1)
    width = left_ref.shape[1]
    own_start = window // HALO
    for c in range(window // tile):
        columns = slice(c * tile, (c + 1) * tile)
        mean = jnp.concatenate(
            [
                jnp.concatenate(
                    [
                        mean_ref[f, (2 * c + e) * channels : (2 * c + e + 1) * channels]
                        for f in range(quarters)
                    ],
                    axis=0,
                )
                for e in range(2)
            ],
            axis=1,
        )
        mean_in = jnp.concatenate(
            [
                dot(
                    atoms_ref[near[f], :, window + inputs : window + inputs + features],
                    mean,
                    LEFT_FIRST,
                ).astype(BF16)
                for f in range(quarters)
            ],
            axis=0,
        )
        pre = dot(states, mean_in, LEFT_FIRST)
        state = jnp.concatenate([atoms_ref[near[f], :, columns] for f in range(quarters)], axis=0)
        updated = (state.astype(F32) + jax.nn.silu(pre)).astype(BF16)
        place = c * tile - own_start
        if 0 <= place < own_start:
            kept[:, place : place + tile] = updated
        table = dot(updated, sides, LEFT_FIRST).astype(BF16)
        table_left[:, c * width : (c + 1) * width] = table[:, :width]
        table_right[:, c * width : (c + 1) * width] = table[:, width:]
    own = pl.multiple_of(feat * features, features)
    atom_out_ref[...] = kept[pl.ds(own, features), :]
    bonds = bonds_ref.shape[0]
    per_quarter = bonds // quarters
    lane = lax.broadcasted_iota(jnp.int32, (tile, tile), 1)
    row = lax.broadcasted_iota(jnp.int32, (BLOCK, width), 0)
    for t in range(bonds // tile):
        rows = slice(t * tile, (t + 1) * tile)
        mixed = None
        for side, table in ((0, table_left), (1, table_right)):
            end = ends_ref[rows, side : side + 1]
            chosen = jnp.where(end % tile == lane, 1.0, 0.0).astype(BF16)
            found = jnp.dot(chosen, table[...], preferred_element_type=F32)
            high = jnp.broadcast_to(end // tile, (tile, width))
            for c in range(window // tile):
                part = jnp.where(high == c, found[:, c * width : (c + 1) * width], 0.0)
                mixed = part if mixed is None else mixed + part
        message = jnp.concatenate(
            [
                jnp.concatenate(
                    [
                        mean_ref[f, after + b * channels : after + (b + 1) * channels]
                        for f in range(quarters)
                    ],
                    axis=0,
                )
                for b in range(t * (tile // BLOCK), (t + 1) * (tile // BLOCK))
            ],
            axis=1,
        )
        gate = dot(message, gate_ref[...], LEFT_FIRST)
        q = t * tile // per_quarter
        start = t * tile - q * per_quarter
        hidden = hidden_ref[near[q], start : start + tile].astype(F32)
        update = jax.nn.sigmoid(gate) * (hidden + jax.nn.silu(mixed))
        for e in range(tile // BLOCK):
            part = slice(e * BLOCK, (e + 1) * BLOCK)
            real = row < fill_ref[t * (tile // BLOCK) + e]
            here = slice(t * tile + e * BLOCK, t * tile + (e + 1) * BLOCK)
            bond_out_ref[here] = (
                bonds_ref[here].astype(F32) + jnp.where(real, update[part], 0.0)
            ).astype(BF16)


def update_call(fill, place, mean, atoms, left, right, gate, hidden, bonds, ends):
    features = atoms.shape[1]
    window = HALO * SPAN * LANES
    width = left.shape[1]
    tile = 2 * LANES
    return pl.pallas_call(
        update_body,
        out_shape=(
            jax.ShapeDtypeStruct(bonds.shape, BF16),
            jax.ShapeDtypeStruct((features, window // HALO), BF16),
        ),
        in_specs=[smem(), smem()] + [vmem()] * 8,
        out_specs=(vmem(), vmem()),
        scratch_shapes=[
            pltpu.VMEM((tile, window // tile * width), BF16),
            pltpu.VMEM((tile, window // tile * width), BF16),
            pltpu.VMEM((mean.shape[0] * features, window // HALO), BF16),
        ],
        cost_estimate=pl.CostEstimate(
            flops=2_500_000_000, bytes_accessed=4_000_000, transcendentals=2_000_000
        ),
        compiler_params=pltpu.CompilerParams(vmem_limit_bytes=ROOM),
        name="update",
    )(fill, place, mean, atoms, left, right, gate, hidden, bonds, ends)


def local(
    bond_state,
    block_fill,
    w_in,
    w_down,
    pair_coef,
    pair_source,
    pair_owner,
    pair_target,
    w_gate,
    w_atom_in,
    atom_state,
    w_atom,
    bond_ends,
    w_left,
    w_right,
):
    spaces = lax.axis_size("space")
    feats = lax.axis_size("feat")
    space = lax.axis_index("space").astype(jnp.int32).reshape(1)
    feat = lax.axis_index("feat").astype(jnp.int32).reshape(1)
    bonds, width = bond_state.shape
    blocks = block_fill.shape[0]
    pairs = pair_source.shape[0]
    channels = w_down.shape[1] // feats
    own_bonds = bonds // feats
    near_groups = [[4 * i + k for k in range(4)] for i in range(spaces // 4)]
    first_of = [4 * i for i in range(spaces // 4)]
    next_pairs = swapped(first_of, spaces, 1)
    over_pairs = swapped([i + k for i in first_of for k in (0, 1)], spaces, 2)
    half = channels // 2
    stride = SLOTS * half + 1

    lower = lax.ppermute(atom_state, "space", [(i, (i + 1) % spaces) for i in range(spaces)])
    upper = lax.ppermute(atom_state, "space", [((i + 1) % spaces, i) for i in range(spaces)])
    parts = (
        bond_state.reshape(feats, own_bonds, width),
        for_each(w_in, "feat"),
        for_each(w_down.T, "feat"),
    )
    entered = exchanged(jnp.concatenate(parts, axis=1), "feat")
    owners = pair_owner[:, 0]
    before = lax.broadcasted_iota(jnp.int32, (pairs, pairs), 1) < lax.broadcasted_iota(
        jnp.int32, (pairs, pairs), 0
    )
    same = before & (owners[:, None] == owners[None, :])
    rank = jnp.sum(jnp.where(same, 1, 0), axis=1)
    slots = owners * stride + rank * half
    flat = owners * SLOTS + rank
    wanted = flat[:, None] == lax.broadcasted_iota(jnp.int32, (pairs, spaces * SLOTS), 1)
    labels = blocks + jnp.sum(jnp.where(wanted, pair_target[:, None] - blocks, 0), axis=0)
    lane = lax.broadcasted_iota(jnp.int32, (spaces, SLOTS, LANES), 2)
    labels = jnp.where(lane == space[0], labels.reshape(spaces, SLOTS, 1), 0).astype(BF16)
    ends = bond_ends.T
    entered, ends, slots, labels = lax.optimization_barrier((entered, ends, slots, labels))
    hidden, angular = angular_call(block_fill, feat, entered, own_bonds, blocks // feats, channels)
    angular = exchanged(angular, "feat")
    angular = angular.reshape(blocks, *angular.shape[2:])
    outgoing = contribution_call(pair_source, slots, labels, angular, pair_coef)
    outgoing, hidden = lax.optimization_barrier((outgoing, hidden))
    arrived = exchanged(outgoing.reshape(spaces, stride, *outgoing.shape[1:]), "space")
    arrived = arrived.reshape(outgoing.shape)
    atoms = jnp.concatenate([lower, atom_state, upper, w_atom, w_atom_in], axis=1)
    turned = [hidden[k] if k == 0 else moved(hidden[k], "feat", k) for k in range(feats)]
    hidden = jnp.stack(turned)
    atoms = jnp.stack(
        [atoms if k == 0 else moved(atoms, "feat", k) for k in range(feats)]
    )
    arrived, hidden, atoms = lax.optimization_barrier((arrived, hidden, atoms))
    message, own, near, beside, over = message_call(block_fill, space, bond_ends, arrived, channels)
    near = exchanged(near, "space", near_groups)
    beside = lax.ppermute(beside, "space", next_pairs)
    over = lax.ppermute(over, "space", over_pairs)
    mean = mean_call(space, own, near, beside, over, message, feats)
    mean = exchanged(mean, "feat")
    return update_call(
        block_fill, feat, mean, atoms, w_left, w_right, w_gate, hidden, bond_state, ends
    )


def solution(mesh):
    placed = (
        P("space", "feat"),
        P("space"),
        P(None, "feat"),
        P("feat", None),
        P("space", None, None),
        P("space"),
        P("space", None),
        P("space"),
        P(None, "feat"),
        P(None, "feat"),
        P("feat", "space"),
        P("feat", None),
        P(None, "space"),
        P(None, "feat"),
        P(None, "feat"),
    )
    return jax.shard_map(
        local,
        mesh=mesh,
        in_specs=placed,
        out_specs=(P("space", "feat"), P("feat", "space")),
        check_vma=False,
    )
```

```python
import functools

import jax
import jax.numpy as jnp
from jax import lax
from jax.experimental import pallas as pl
from jax.experimental.pallas import tpu as pltpu
from jax.sharding import PartitionSpec as P


BF16 = jnp.bfloat16
F32 = jnp.float32
BLOCK = 128
LANES = 128
SLOTS = 2
SPAN = 4
HALO = 3
ROOM = 24 << 20
WIDE = 58 << 20
LEFT_FIRST = (((0,), (0,)), ((), ()))
BOTH_LAST = (((1,), (1,)), ((), ()))


def vmem():
    return pl.BlockSpec(memory_space=pltpu.VMEM)


def smem():
    return pl.BlockSpec(memory_space=pltpu.SMEM)


def dot(a, b, dims):
    return lax.dot_general(a, b, dims, preferred_element_type=F32)


def exchanged(value, axis, groups=None):
    return lax.all_to_all(
        value, axis, split_axis=0, concat_axis=0, tiled=True, axis_index_groups=groups
    )


def moved(value, axis, steps):
    count = lax.axis_size(axis)
    return lax.ppermute(value, axis, [(i, (i + steps) % count) for i in range(count)])


def swapped(places, count, step):
    out = []
    for place in places:
        below = (place - step) % count
        out += [(place, below), (below, place)]
    return out


def entry_body(x_hbm, w_hbm, down_ref, out_ref, sems):
    quarters = out_ref.shape[0]
    bonds = x_hbm.shape[0] // quarters
    inputs = w_hbm.shape[0]
    copies = []
    for q in range(quarters):
        copies.append(
            pltpu.make_async_copy(
                x_hbm.at[pl.ds(q * bonds, bonds)], out_ref.at[q, pl.ds(0, bonds)], sems.at[2 * q]
            )
        )
        copies.append(
            pltpu.make_async_copy(w_hbm, out_ref.at[q, pl.ds(bonds, inputs)], sems.at[2 * q + 1])
        )
    for copy in copies:
        copy.start()
    down = down_ref[...].astype(F32).T.astype(BF16)
    for q in range(quarters):
        out_ref[q, bonds + inputs :] = down
    for copy in copies:
        copy.wait()


def entry_call(x, w, down, quarters):
    bonds, width = x.shape
    rows = bonds // quarters + w.shape[0] + down.shape[1]
    return pl.pallas_call(
        entry_body,
        out_shape=jax.ShapeDtypeStruct((quarters, rows, width), BF16),
        in_specs=[
            pl.BlockSpec(memory_space=pl.ANY),
            pl.BlockSpec(memory_space=pl.ANY),
            vmem(),
        ],
        out_specs=vmem(),
        scratch_shapes=[pltpu.SemaphoreType.DMA((2 * quarters,))],
        cost_estimate=pl.CostEstimate(flops=0, bytes_accessed=2_000_000, transcendentals=0),
        compiler_params=pltpu.CompilerParams(vmem_limit_bytes=WIDE),
        name="entry",
    )(x, w, down)


def angular_body(fill_ref, place_ref, pack_ref, hidden_ref, angular_ref):
    quarters, own_blocks, channels = angular_ref.shape[:3]
    bonds, width = hidden_ref.shape[1:]
    inputs = quarters * width
    feat = place_ref[0]
    first = feat * own_blocks
    x = jnp.concatenate([pack_ref[k, :bonds] for k in range(quarters)], axis=1)
    total = None
    for q in range(quarters):
        pre = jnp.dot(x, pack_ref[q, bonds : bonds + inputs], preferred_element_type=F32)
        hidden = jax.nn.silu(pre).astype(BF16)
        hidden_ref[(q - feat + quarters) % quarters] = hidden
        part = dot(pack_ref[q, bonds + inputs :], hidden, BOTH_LAST)
        total = part if total is None else total + part
    for b in range(own_blocks):
        piece = total[:, b * BLOCK : (b + 1) * BLOCK]
        real = lax.broadcasted_iota(jnp.int32, piece.shape, 1) < fill_ref[first + b]
        piece = jnp.where(real, piece, 0.0).astype(BF16)
        for q in range(quarters):
            angular_ref[q, b] = piece[q * channels : (q + 1) * channels]


def angular_call(fill, place, pack, bonds, own_blocks, channels):
    quarters, _, width = pack.shape
    return pl.pallas_call(
        angular_body,
        out_shape=(
            jax.ShapeDtypeStruct((quarters, bonds, width), BF16),
            jax.ShapeDtypeStruct((quarters, own_blocks, channels, BLOCK), BF16),
        ),
        in_specs=[smem(), smem(), vmem()],
        out_specs=(vmem(), vmem()),
        cost_estimate=pl.CostEstimate(
            flops=600_000_000, bytes_accessed=2_000_000, transcendentals=262_144
        ),
        compiler_params=pltpu.CompilerParams(vmem_limit_bytes=ROOM),
        name="angular",
    )(fill, place, pack)


def contribution_body(
    chunks, group, source_ref, slot_ref, label_ref, angular_ref, coef_hbm, out_ref, coef_ref, sems
):
    channels, rows = angular_ref.shape[1:]
    half = channels // 2
    stride = SLOTS * half + 1
    per_chunk = coef_ref.shape[0] // chunks
    copies = []
    for c in range(chunks):
        here = pl.ds(c * per_chunk, per_chunk)
        copies.append(pltpu.make_async_copy(coef_hbm.at[here], coef_ref.at[here], sems.at[c]))
        copies[c].start()
    out_ref[...] = jnp.zeros_like(out_ref)

    def tag(step, carry):
        for k in range(4):
            owner = step * 4 + k
            out_ref[owner * stride + stride - 1] = label_ref[owner]
        return carry

    lax.fori_loop(0, label_ref.shape[0] // 4, tag, 0)
    blank = jnp.zeros((channels, rows), BF16)
    for c in range(chunks):
        copies[c].wait()
        for first in range(c * per_chunk, (c + 1) * per_chunk, group):
            pairs = range(first, first + group)
            left = []
            right = []
            for k, pair in enumerate(pairs):
                value = angular_ref[source_ref[pair]]
                sides = [value, blank] if k % 2 == 0 else [blank, value]
                left.append(jnp.concatenate(sides, axis=1))
            for k in range(0, group, 2):
                sides = [coef_ref[first + k], coef_ref[first + k + 1]]
                right.append(jnp.concatenate(sides, axis=1))
            found = dot(jnp.concatenate(left, axis=0), jnp.concatenate(right, axis=0), BOTH_LAST)
            for k, pair in enumerate(pairs):
                column = k // 2 * rows
                part = found[k * channels : (k + 1) * channels, column : column + rows]
                part = part.astype(BF16).reshape(half, 2, rows)
                out_ref[pl.ds(slot_ref[pair], half)] = part


def contribution_call(sources, slots, labels, angular, coef):
    pairs = coef.shape[0]
    chunks, group = next(
        (c, g) for g in (4, 2) for c in (4, 2, 1) if pairs % (c * g) == 0
    )
    _, channels, rows = angular.shape
    stride = SLOTS * channels // 2 + 1
    return pl.pallas_call(
        functools.partial(contribution_body, chunks, group),
        out_shape=jax.ShapeDtypeStruct((labels.shape[0] * stride, 2, rows), BF16),
        in_specs=[
            smem(),
            smem(),
            vmem(),
            vmem(),
            pl.BlockSpec(memory_space=pltpu.HBM),
        ],
        out_specs=vmem(),
        scratch_shapes=[
            pltpu.VMEM(coef.shape, BF16),
            pltpu.SemaphoreType.DMA((chunks,)),
        ],
        cost_estimate=pl.CostEstimate(
            flops=60_000_000, bytes_accessed=5_000_000, transcendentals=0
        ),
        compiler_params=pltpu.CompilerParams(vmem_limit_bytes=WIDE),
        name="contribution",
    )(sources, slots, labels, angular, coef)


def message_body(
    fill_ref,
    place_ref,
    ends_ref,
    arrived_ref,
    message_ref,
    own_ref,
    near_ref,
    next_ref,
    over_ref,
    sums,
    padded,
    labels,
    label_ref,
    sem,
):
    blocks = fill_ref.shape[0]
    channels, rows = sums.shape[1:]
    half = channels // 2
    stride = SLOTS * half + 1
    sources = arrived_ref.shape[0] // stride
    bonds = blocks * rows
    spans = HALO * SPAN
    total = jnp.zeros((2, rows), F32)
    for source in range(sources):
        total += arrived_ref[source * stride + stride - 1].astype(F32)
    labels[...] = total.astype(jnp.int32)
    copy = pltpu.make_async_copy(labels, label_ref, sem)
    copy.start()
    sums[...] = jnp.zeros_like(sums)
    copy.wait()

    def add(step, carry):
        for k in range(4):
            source = step * 4 + k
            for slot in range(SLOTS):
                part = arrived_ref[pl.ds(source * stride + slot * half, half)]
                sums[label_ref[slot, source]] += part.reshape(channels, rows).astype(F32)
        return carry

    lax.fori_loop(0, sources // 4, add, 0)
    pieces = []
    masks = []
    for b in range(blocks):
        real = lax.broadcasted_iota(jnp.int32, (channels, rows), 1) < fill_ref[b]
        piece = jnp.where(real, sums[b], 0.0)
        message_ref[b * channels : (b + 1) * channels] = piece.astype(BF16)
        pieces.append(piece)
        masks.append(jnp.where(real[:1], 1.0, 0.0))
    message = jnp.concatenate(pieces, axis=1)
    mask = jnp.concatenate(masks, axis=1)
    ends = ends_ref[1:2, :]
    high = ends // LANES
    low = ends % LANES
    stacked = []
    tallies = []
    for h in range(spans):
        here = high == h
        stacked.append(jnp.where(here, message, 0.0).astype(BF16))
        tallies.append(jnp.where(here, mask, 0.0))
    tallies.append(jnp.zeros((16 - spans, bonds), F32))
    stacked.append(jnp.concatenate(tallies, axis=0).astype(BF16))
    chosen = jnp.where(
        low == lax.broadcasted_iota(jnp.int32, (LANES, bonds), 0), 1.0, 0.0
    ).astype(BF16)
    window = dot(jnp.concatenate(stacked, axis=0), chosen, BOTH_LAST)
    counts = window[spans * channels : spans * channels + spans]
    upper = jnp.floor(counts * (1.0 / 256.0))
    lower = counts - 256.0 * upper
    padded[...] = jnp.zeros_like(padded)
    width = SPAN * channels
    for k in range(HALO):
        group = jnp.concatenate(
            [
                window[k * width : (k + 1) * width],
                upper[k * SPAN : (k + 1) * SPAN],
                lower[k * SPAN : (k + 1) * SPAN],
            ],
            axis=0,
        )
        own_ref[k] = group
        padded[HALO + k] = group.astype(BF16)
    near = place_ref[0] % 4
    for m in range(4):
        start = jnp.where(m == near, 0, m - near + HALO)
        for k in range(HALO):
            near_ref[m, k] = padded[start + k]
    first = HALO + jnp.where(near == 3, 1, 0)
    next_ref[0] = padded[first]
    next_ref[1] = padded[first + 1]
    over_ref[...] = padded[HALO + jnp.where(near >= 2, 2, 0)]


def message_call(fill, place, ends, arrived, channels):
    rows = arrived.shape[2]
    blocks = fill.shape[0]
    depth = SPAN * channels + 2 * SPAN
    return pl.pallas_call(
        message_body,
        out_shape=(
            jax.ShapeDtypeStruct((blocks * channels, rows), BF16),
            jax.ShapeDtypeStruct((HALO, depth, LANES), F32),
            jax.ShapeDtypeStruct((4, HALO, depth, LANES), BF16),
            jax.ShapeDtypeStruct((2, depth, LANES), BF16),
            jax.ShapeDtypeStruct((depth, LANES), BF16),
        ),
        in_specs=[smem(), smem(), vmem(), vmem()],
        out_specs=(vmem(), vmem(), vmem(), vmem(), vmem()),
        scratch_shapes=[
            pltpu.VMEM((blocks + 1, channels, rows), F32),
            pltpu.VMEM((3 * HALO, depth, LANES), BF16),
            pltpu.VMEM((SLOTS, LANES), jnp.int32),
            pltpu.SMEM((SLOTS, LANES), jnp.int32),
            pltpu.SemaphoreType.DMA(()),
        ],
        cost_estimate=pl.CostEstimate(
            flops=120_000_000, bytes_accessed=2_000_000, transcendentals=0
        ),
        compiler_params=pltpu.CompilerParams(vmem_limit_bytes=ROOM),
        name="message",
    )(fill, place, ends, arrived)


def mean_body(place_ref, own_ref, near_ref, next_ref, over_ref, message_ref, out_ref, total):
    copies = out_ref.shape[0]
    depth = own_ref.shape[1]
    channels = (depth - 2 * SPAN) // SPAN
    width = SPAN * channels
    spot = place_ref[0] % 4
    for k in range(HALO):
        value = own_ref[k]
        for m in range(4):
            value += near_ref[m, k].astype(F32)
        total[k] = value
    first = jnp.where(spot == 3, 1, 0)
    total[first] += next_ref[0].astype(F32)
    total[first + 1] += next_ref[1].astype(F32)
    total[jnp.where(spot >= 2, 2, 0)] += over_ref[...].astype(F32)
    for k in range(HALO):
        value = total[k]
        for h in range(SPAN):
            count = 256.0 * value[width + h : width + h + 1]
            count += value[width + SPAN + h : width + SPAN + h + 1]
            mean = value[h * channels : (h + 1) * channels] / jnp.maximum(count, 1.0)
            mean = mean.astype(BF16)
            row = (k * SPAN + h) * channels
            for m in range(copies):
                out_ref[m, row : row + channels] = mean
    for m in range(copies):
        out_ref[m, HALO * width :] = message_ref[...]


def mean_call(place, own, near, beside, over, message, copies):
    depth = own.shape[1]
    width = depth - 2 * SPAN
    rows = HALO * width + message.shape[0]
    return pl.pallas_call(
        mean_body,
        out_shape=jax.ShapeDtypeStruct((copies, rows, LANES), BF16),
        in_specs=[smem()] + [vmem()] * 5,
        out_specs=vmem(),
        scratch_shapes=[pltpu.VMEM((HALO, depth, LANES), F32)],
        cost_estimate=pl.CostEstimate(
            flops=1_000_000, bytes_accessed=600_000, transcendentals=0
        ),
        compiler_params=pltpu.CompilerParams(vmem_limit_bytes=ROOM),
        name="mean",
    )(place, own, near, beside, over, message)


def update_body(
    fill_ref,
    place_ref,
    mean_ref,
    atoms_ref,
    left_ref,
    right_ref,
    gate_ref,
    hidden_ref,
    bonds_ref,
    ends_ref,
    bond_out_ref,
    atom_out_ref,
    table_left,
    table_right,
    kept,
):
    quarters = mean_ref.shape[0]
    channels = gate_ref.shape[0] // quarters
    feat = place_ref[0]
    near = [(feat - q + quarters) % quarters for q in range(quarters)]
    after = HALO * SPAN * channels
    features = atoms_ref.shape[1]
    window = HALO * SPAN * LANES
    inputs = quarters * features
    tile = 2 * LANES
    states = jnp.concatenate(
        [atoms_ref[near[f], :, window : window + inputs] for f in range(quarters)], axis=0
    )
    sides = jnp.concatenate([left_ref[...], right_ref[...]], axis=1)
    width = left_ref.shape[1]
    own_start = window // HALO
    for c in range(window // tile):
        columns = slice(c * tile, (c + 1) * tile)
        mean = jnp.concatenate(
            [
                jnp.concatenate(
                    [
                        mean_ref[f, (2 * c + e) * channels : (2 * c + e + 1) * channels]
                        for f in range(quarters)
                    ],
                    axis=0,
                )
                for e in range(2)
            ],
            axis=1,
        )
        mean_in = jnp.concatenate(
            [
                dot(
                    atoms_ref[near[f], :, window + inputs : window + inputs + features],
                    mean,
                    LEFT_FIRST,
                ).astype(BF16)
                for f in range(quarters)
            ],
            axis=0,
        )
        pre = dot(states, mean_in, LEFT_FIRST)
        state = jnp.concatenate([atoms_ref[near[f], :, columns] for f in range(quarters)], axis=0)
        updated = (state.astype(F32) + jax.nn.silu(pre)).astype(BF16)
        place = c * tile - own_start
        if 0 <= place < own_start:
            kept[:, place : place + tile] = updated
        table = dot(updated, sides, LEFT_FIRST).astype(BF16)
        table_left[:, c * width : (c + 1) * width] = table[:, :width]
        table_right[:, c * width : (c + 1) * width] = table[:, width:]
    own = pl.multiple_of(feat * features, features)
    atom_out_ref[...] = kept[pl.ds(own, features), :]
    bonds = bonds_ref.shape[0]
    per_quarter = bonds // quarters
    lane = lax.broadcasted_iota(jnp.int32, (tile, tile), 1)
    row = lax.broadcasted_iota(jnp.int32, (BLOCK, width), 0)
    for t in range(bonds // tile):
        rows = slice(t * tile, (t + 1) * tile)
        mixed = None
        for side, table in ((0, table_left), (1, table_right)):
            end = ends_ref[rows, side : side + 1]
            chosen = jnp.where(end % tile == lane, 1.0, 0.0).astype(BF16)
            found = jnp.dot(chosen, table[...], preferred_element_type=F32)
            high = jnp.broadcast_to(end // tile, (tile, width))
            for c in range(window // tile):
                part = jnp.where(high == c, found[:, c * width : (c + 1) * width], 0.0)
                mixed = part if mixed is None else mixed + part
        message = jnp.concatenate(
            [
                jnp.concatenate(
                    [
                        mean_ref[f, after + b * channels : after + (b + 1) * channels]
                        for f in range(quarters)
                    ],
                    axis=0,
                )
                for b in range(t * (tile // BLOCK), (t + 1) * (tile // BLOCK))
            ],
            axis=1,
        )
        gate = dot(message, gate_ref[...], LEFT_FIRST)
        q = t * tile // per_quarter
        start = t * tile - q * per_quarter
        hidden = hidden_ref[near[q], start : start + tile].astype(F32)
        update = jax.nn.sigmoid(gate) * (hidden + jax.nn.silu(mixed))
        for e in range(tile // BLOCK):
            part = slice(e * BLOCK, (e + 1) * BLOCK)
            real = row < fill_ref[t * (tile // BLOCK) + e]
            here = slice(t * tile + e * BLOCK, t * tile + (e + 1) * BLOCK)
            bond_out_ref[here] = (
                bonds_ref[here].astype(F32) + jnp.where(real, update[part], 0.0)
            ).astype(BF16)


def update_call(fill, place, mean, atoms, left, right, gate, hidden, bonds, ends):
    features = atoms.shape[1]
    window = HALO * SPAN * LANES
    width = left.shape[1]
    tile = 2 * LANES
    return pl.pallas_call(
        update_body,
        out_shape=(
            jax.ShapeDtypeStruct(bonds.shape, BF16),
            jax.ShapeDtypeStruct((features, window // HALO), BF16),
        ),
        in_specs=[smem(), smem()] + [vmem()] * 8,
        out_specs=(vmem(), vmem()),
        scratch_shapes=[
            pltpu.VMEM((tile, window // tile * width), BF16),
            pltpu.VMEM((tile, window // tile * width), BF16),
            pltpu.VMEM((mean.shape[0] * features, window // HALO), BF16),
        ],
        cost_estimate=pl.CostEstimate(
            flops=2_500_000_000, bytes_accessed=4_000_000, transcendentals=2_000_000
        ),
        compiler_params=pltpu.CompilerParams(vmem_limit_bytes=ROOM),
        name="update",
    )(fill, place, mean, atoms, left, right, gate, hidden, bonds, ends)


def local(
    bond_state,
    block_fill,
    w_in,
    w_down,
    pair_coef,
    pair_source,
    pair_owner,
    pair_target,
    w_gate,
    w_atom_in,
    atom_state,
    w_atom,
    bond_ends,
    w_left,
    w_right,
):
    spaces = lax.axis_size("space")
    feats = lax.axis_size("feat")
    space = lax.axis_index("space").astype(jnp.int32).reshape(1)
    feat = lax.axis_index("feat").astype(jnp.int32).reshape(1)
    bonds, _ = bond_state.shape
    blocks = block_fill.shape[0]
    pairs = pair_source.shape[0]
    channels = w_down.shape[1] // feats
    own_bonds = bonds // feats
    near_groups = [[4 * i + k for k in range(4)] for i in range(spaces // 4)]
    first_of = [4 * i for i in range(spaces // 4)]
    next_pairs = swapped(first_of, spaces, 1)
    over_pairs = swapped([i + k for i in first_of for k in (0, 1)], spaces, 2)
    half = channels // 2
    stride = SLOTS * half + 1

    lower = lax.ppermute(atom_state, "space", [(i, (i + 1) % spaces) for i in range(spaces)])
    upper = lax.ppermute(atom_state, "space", [((i + 1) % spaces, i) for i in range(spaces)])
    entered = entry_call(bond_state, w_in, w_down, feats)
    entered = exchanged(entered, "feat")
    owners = pair_owner[:, 0]
    before = lax.broadcasted_iota(jnp.int32, (pairs, pairs), 1) < lax.broadcasted_iota(
        jnp.int32, (pairs, pairs), 0
    )
    same = before & (owners[:, None] == owners[None, :])
    rank = jnp.sum(jnp.where(same, 1, 0), axis=1)
    slots = owners * stride + rank * half
    flat = owners * SLOTS + rank
    wanted = flat[:, None] == lax.broadcasted_iota(jnp.int32, (pairs, spaces * SLOTS), 1)
    labels = blocks + jnp.sum(jnp.where(wanted, pair_target[:, None] - blocks, 0), axis=0)
    lane = lax.broadcasted_iota(jnp.int32, (spaces, SLOTS, LANES), 2)
    labels = jnp.where(lane == space[0], labels.reshape(spaces, SLOTS, 1), 0).astype(BF16)
    ends = bond_ends.T
    entered, ends, slots, labels = lax.optimization_barrier((entered, ends, slots, labels))
    hidden, angular = angular_call(block_fill, feat, entered, own_bonds, blocks // feats, channels)
    angular = exchanged(angular, "feat")
    angular, lower, upper = lax.optimization_barrier((angular, lower, upper))
    angular = angular.reshape(blocks, *angular.shape[2:])
    outgoing = contribution_call(pair_source, slots, labels, angular, pair_coef)
    outgoing, hidden = lax.optimization_barrier((outgoing, hidden))
    arrived = exchanged(outgoing.reshape(spaces, stride, *outgoing.shape[1:]), "space")
    arrived = arrived.reshape(outgoing.shape)
    atoms = jnp.concatenate([lower, atom_state, upper, w_atom, w_atom_in], axis=1)
    turned = [hidden[k] if k == 0 else moved(hidden[k], "feat", k) for k in range(feats)]
    hidden = jnp.stack(turned)
    atoms = jnp.stack(
        [atoms if k == 0 else moved(atoms, "feat", k) for k in range(feats)]
    )
    arrived, hidden, atoms = lax.optimization_barrier((arrived, hidden, atoms))
    message, own, near, beside, over = message_call(block_fill, space, bond_ends, arrived, channels)
    near = exchanged(near, "space", near_groups)
    beside = lax.ppermute(beside, "space", next_pairs)
    over = lax.ppermute(over, "space", over_pairs)
    mean = mean_call(space, own, near, beside, over, message, feats)
    mean = exchanged(mean, "feat")
    return update_call(
        block_fill, feat, mean, atoms, w_left, w_right, w_gate, hidden, bond_state, ends
    )


def solution(mesh):
    placed = (
        P("space", "feat"),
        P("space"),
        P(None, "feat"),
        P("feat", None),
        P("space", None, None),
        P("space"),
        P("space", None),
        P("space"),
        P(None, "feat"),
        P(None, "feat"),
        P("feat", "space"),
        P("feat", None),
        P(None, "space"),
        P(None, "feat"),
        P(None, "feat"),
    )
    return jax.shard_map(
        local,
        mesh=mesh,
        in_specs=placed,
        out_specs=(P("space", "feat"), P("feat", "space")),
        check_vma=False,
    )
```

```python
import functools

import jax
import jax.numpy as jnp
from jax import lax
from jax.experimental import pallas as pl
from jax.experimental.pallas import tpu as pltpu
from jax.sharding import PartitionSpec as P


BF16 = jnp.bfloat16
F32 = jnp.float32
BLOCK = 128
LANES = 128
SLOTS = 2
SPAN = 4
HALO = 3
ROOM = 24 << 20
WIDE = 58 << 20
LEFT_FIRST = (((0,), (0,)), ((), ()))
BOTH_LAST = (((1,), (1,)), ((), ()))


def vmem():
    return pl.BlockSpec(memory_space=pltpu.VMEM)


def smem():
    return pl.BlockSpec(memory_space=pltpu.SMEM)


def dot(a, b, dims):
    return lax.dot_general(a, b, dims, preferred_element_type=F32)


def exchanged(value, axis, groups=None):
    return lax.all_to_all(
        value, axis, split_axis=0, concat_axis=0, tiled=True, axis_index_groups=groups
    )


def moved(value, axis, steps):
    count = lax.axis_size(axis)
    return lax.ppermute(value, axis, [(i, (i + steps) % count) for i in range(count)])


def swapped(places, count, step):
    out = []
    for place in places:
        below = (place - step) % count
        out += [(place, below), (below, place)]
    return out


def entry_body(x_hbm, w_hbm, down_ref, out_hbm, x_ref, w_ref, load_sems, store_sems):
    quarters, rows = x_ref.shape[:2]
    inputs = w_ref.shape[0]
    loads = [pltpu.make_async_copy(w_hbm, w_ref, load_sems.at[quarters])]
    for q in range(quarters):
        here = x_hbm.at[pl.ds(q * rows, rows)]
        loads.append(pltpu.make_async_copy(here, x_ref.at[q], load_sems.at[q]))
    for load in loads:
        load.start()
    stores = []

    def store(source, q, first, kind):
        there = out_hbm.at[q, pl.ds(first, source.shape[0])]
        stores.append(pltpu.make_async_copy(source, there, store_sems.at[3 * q + kind]))
        stores[-1].start()

    for q in range(quarters):
        store(down_ref, q, rows + inputs, 0)
    loads[0].wait()
    for q in range(quarters):
        store(w_ref, q, rows, 1)
    for q in range(quarters):
        loads[1 + q].wait()
        store(x_ref.at[q], q, 0, 2)
    for copy in stores:
        copy.wait()


def entry_call(x, w, down, quarters):
    bonds, width = x.shape
    rows = bonds // quarters
    return pl.pallas_call(
        entry_body,
        out_shape=jax.ShapeDtypeStruct((quarters, rows + w.shape[0] + down.shape[0], width), BF16),
        in_specs=[
            pl.BlockSpec(memory_space=pl.ANY),
            pl.BlockSpec(memory_space=pl.ANY),
            vmem(),
        ],
        out_specs=pl.BlockSpec(memory_space=pl.ANY),
        scratch_shapes=[
            pltpu.VMEM((quarters, rows, width), BF16),
            pltpu.VMEM(w.shape, BF16),
            pltpu.SemaphoreType.DMA((quarters + 1,)),
            pltpu.SemaphoreType.DMA((3 * quarters,)),
        ],
        cost_estimate=pl.CostEstimate(flops=0, bytes_accessed=2_000_000, transcendentals=0),
        compiler_params=pltpu.CompilerParams(vmem_limit_bytes=WIDE),
        name="entry",
    )(x, w, down)


def angular_body(fill_ref, place_ref, pack_ref, hidden_ref, angular_ref):
    quarters, own_blocks, channels = angular_ref.shape[:3]
    bonds, width = hidden_ref.shape[1:]
    inputs = quarters * width
    feat = place_ref[0]
    first = feat * own_blocks
    x = jnp.concatenate([pack_ref[k, :bonds] for k in range(quarters)], axis=1)
    total = None
    for q in range(quarters):
        pre = jnp.dot(x, pack_ref[q, bonds : bonds + inputs], preferred_element_type=F32)
        hidden = jax.nn.silu(pre).astype(BF16)
        hidden_ref[(q - feat + quarters) % quarters] = hidden
        part = dot(pack_ref[q, bonds + inputs :], hidden, BOTH_LAST)
        total = part if total is None else total + part
    for b in range(own_blocks):
        piece = total[:, b * BLOCK : (b + 1) * BLOCK]
        real = lax.broadcasted_iota(jnp.int32, piece.shape, 1) < fill_ref[first + b]
        piece = jnp.where(real, piece, 0.0).astype(BF16)
        for q in range(quarters):
            angular_ref[q, b] = piece[q * channels : (q + 1) * channels]


def angular_call(fill, place, pack, bonds, own_blocks, channels):
    quarters, _, width = pack.shape
    return pl.pallas_call(
        angular_body,
        out_shape=(
            jax.ShapeDtypeStruct((quarters, bonds, width), BF16),
            jax.ShapeDtypeStruct((quarters, own_blocks, channels, BLOCK), BF16),
        ),
        in_specs=[smem(), smem(), vmem()],
        out_specs=(vmem(), vmem()),
        cost_estimate=pl.CostEstimate(
            flops=600_000_000, bytes_accessed=2_000_000, transcendentals=262_144
        ),
        compiler_params=pltpu.CompilerParams(vmem_limit_bytes=ROOM),
        name="angular",
    )(fill, place, pack)


def contribution_body(
    chunks, group, source_ref, slot_ref, label_ref, angular_ref, coef_hbm, out_ref, coef_ref, sems
):
    channels, rows = angular_ref.shape[1:]
    half = channels // 2
    stride = SLOTS * half + 1
    per_chunk = coef_ref.shape[0] // chunks
    copies = []
    for c in range(chunks):
        here = pl.ds(c * per_chunk, per_chunk)
        copies.append(pltpu.make_async_copy(coef_hbm.at[here], coef_ref.at[here], sems.at[c]))
        copies[c].start()
    out_ref[...] = jnp.zeros_like(out_ref)

    def tag(step, carry):
        for k in range(4):
            owner = step * 4 + k
            out_ref[owner * stride + stride - 1] = label_ref[owner]
        return carry

    lax.fori_loop(0, label_ref.shape[0] // 4, tag, 0)
    blank = jnp.zeros((channels, rows), BF16)
    for c in range(chunks):
        copies[c].wait()
        for first in range(c * per_chunk, (c + 1) * per_chunk, group):
            pairs = range(first, first + group)
            left = []
            right = []
            for k, pair in enumerate(pairs):
                value = angular_ref[source_ref[pair]]
                sides = [value, blank] if k % 2 == 0 else [blank, value]
                left.append(jnp.concatenate(sides, axis=1))
            for k in range(0, group, 2):
                sides = [coef_ref[first + k], coef_ref[first + k + 1]]
                right.append(jnp.concatenate(sides, axis=1))
            found = dot(jnp.concatenate(left, axis=0), jnp.concatenate(right, axis=0), BOTH_LAST)
            for k, pair in enumerate(pairs):
                column = k // 2 * rows
                part = found[k * channels : (k + 1) * channels, column : column + rows]
                part = part.astype(BF16).reshape(half, 2, rows)
                out_ref[pl.ds(slot_ref[pair], half)] = part


def contribution_call(sources, slots, labels, angular, coef):
    pairs = coef.shape[0]
    chunks, group = next(
        (c, g) for g in (4, 2) for c in (4, 2, 1) if pairs % (c * g) == 0
    )
    _, channels, rows = angular.shape
    stride = SLOTS * channels // 2 + 1
    return pl.pallas_call(
        functools.partial(contribution_body, chunks, group),
        out_shape=jax.ShapeDtypeStruct((labels.shape[0] * stride, 2, rows), BF16),
        in_specs=[
            smem(),
            smem(),
            vmem(),
            vmem(),
            pl.BlockSpec(memory_space=pltpu.HBM),
        ],
        out_specs=vmem(),
        scratch_shapes=[
            pltpu.VMEM(coef.shape, BF16),
            pltpu.SemaphoreType.DMA((chunks,)),
        ],
        cost_estimate=pl.CostEstimate(
            flops=60_000_000, bytes_accessed=5_000_000, transcendentals=0
        ),
        compiler_params=pltpu.CompilerParams(vmem_limit_bytes=WIDE),
        name="contribution",
    )(sources, slots, labels, angular, coef)


def message_body(
    fill_ref,
    place_ref,
    ends_ref,
    arrived_ref,
    message_ref,
    own_ref,
    near_ref,
    next_ref,
    over_ref,
    sums,
    padded,
    chosen,
    labels,
    label_ref,
    sem,
):
    blocks = fill_ref.shape[0]
    channels, rows = sums.shape[1:]
    half = channels // 2
    stride = SLOTS * half + 1
    sources = arrived_ref.shape[0] // stride
    bonds = blocks * rows
    spans = HALO * SPAN
    total = jnp.zeros((2, rows), F32)
    for source in range(sources):
        total += arrived_ref[source * stride + stride - 1].astype(F32)
    labels[...] = total.astype(jnp.int32)
    copy = pltpu.make_async_copy(labels, label_ref, sem)
    copy.start()
    sums[...] = jnp.zeros_like(sums)
    ends = ends_ref[1:2, :]
    high = ends // LANES
    low = ends % LANES
    chosen[...] = jnp.where(
        low == lax.broadcasted_iota(jnp.int32, (LANES, bonds), 0), 1.0, 0.0
    ).astype(BF16)
    copy.wait()

    def add(step, carry):
        for k in range(4):
            source = step * 4 + k
            for slot in range(SLOTS):
                part = arrived_ref[pl.ds(source * stride + slot * half, half)]
                sums[label_ref[slot, source]] += part.reshape(channels, rows).astype(F32)
        return carry

    lax.fori_loop(0, sources // 4, add, 0)
    pieces = []
    masks = []
    for b in range(blocks):
        real = lax.broadcasted_iota(jnp.int32, (channels, rows), 1) < fill_ref[b]
        piece = jnp.where(real, sums[b], 0.0)
        message_ref[b * channels : (b + 1) * channels] = piece.astype(BF16)
        pieces.append(piece)
        masks.append(jnp.where(real[:1], 1.0, 0.0))
    message = jnp.concatenate(pieces, axis=1)
    mask = jnp.concatenate(masks, axis=1)
    stacked = []
    tallies = []
    for h in range(spans):
        here = high == h
        stacked.append(jnp.where(here, message, 0.0).astype(BF16))
        tallies.append(jnp.where(here, mask, 0.0))
    tallies.append(jnp.zeros((16 - spans, bonds), F32))
    stacked.append(jnp.concatenate(tallies, axis=0).astype(BF16))
    window = dot(jnp.concatenate(stacked, axis=0), chosen[...], BOTH_LAST)
    counts = window[spans * channels : spans * channels + spans]
    upper = jnp.floor(counts * (1.0 / 256.0))
    lower = counts - 256.0 * upper
    padded[...] = jnp.zeros_like(padded)
    width = SPAN * channels
    for k in range(HALO):
        group = jnp.concatenate(
            [
                window[k * width : (k + 1) * width],
                upper[k * SPAN : (k + 1) * SPAN],
                lower[k * SPAN : (k + 1) * SPAN],
            ],
            axis=0,
        )
        own_ref[k] = group
        padded[HALO + k] = group.astype(BF16)
    near = place_ref[0] % 4
    for m in range(4):
        start = jnp.where(m == near, 0, m - near + HALO)
        for k in range(HALO):
            near_ref[m, k] = padded[start + k]
    first = HALO + jnp.where(near == 3, 1, 0)
    next_ref[0] = padded[first]
    next_ref[1] = padded[first + 1]
    over_ref[...] = padded[HALO + jnp.where(near >= 2, 2, 0)]


def message_call(fill, place, ends, arrived, channels):
    rows = arrived.shape[2]
    blocks = fill.shape[0]
    depth = SPAN * channels + 2 * SPAN
    return pl.pallas_call(
        message_body,
        out_shape=(
            jax.ShapeDtypeStruct((blocks * channels, rows), BF16),
            jax.ShapeDtypeStruct((HALO, depth, LANES), F32),
            jax.ShapeDtypeStruct((4, HALO, depth, LANES), BF16),
            jax.ShapeDtypeStruct((2, depth, LANES), BF16),
            jax.ShapeDtypeStruct((depth, LANES), BF16),
        ),
        in_specs=[smem(), smem(), vmem(), vmem()],
        out_specs=(vmem(), vmem(), vmem(), vmem(), vmem()),
        scratch_shapes=[
            pltpu.VMEM((blocks + 1, channels, rows), F32),
            pltpu.VMEM((3 * HALO, depth, LANES), BF16),
            pltpu.VMEM((LANES, blocks * rows), BF16),
            pltpu.VMEM((SLOTS, LANES), jnp.int32),
            pltpu.SMEM((SLOTS, LANES), jnp.int32),
            pltpu.SemaphoreType.DMA(()),
        ],
        cost_estimate=pl.CostEstimate(
            flops=120_000_000, bytes_accessed=2_000_000, transcendentals=0
        ),
        compiler_params=pltpu.CompilerParams(vmem_limit_bytes=ROOM),
        name="message",
    )(fill, place, ends, arrived)


def mean_body(place_ref, own_ref, near_ref, next_ref, over_ref, message_ref, out_ref, total):
    copies = out_ref.shape[0]
    depth = own_ref.shape[1]
    channels = (depth - 2 * SPAN) // SPAN
    width = SPAN * channels
    spot = place_ref[0] % 4
    for k in range(HALO):
        value = own_ref[k]
        for m in range(4):
            value += near_ref[m, k].astype(F32)
        total[k] = value
    first = jnp.where(spot == 3, 1, 0)
    total[first] += next_ref[0].astype(F32)
    total[first + 1] += next_ref[1].astype(F32)
    total[jnp.where(spot >= 2, 2, 0)] += over_ref[...].astype(F32)
    for k in range(HALO):
        value = total[k]
        for h in range(SPAN):
            count = 256.0 * value[width + h : width + h + 1]
            count += value[width + SPAN + h : width + SPAN + h + 1]
            mean = value[h * channels : (h + 1) * channels] / jnp.maximum(count, 1.0)
            mean = mean.astype(BF16)
            row = (k * SPAN + h) * channels
            for m in range(copies):
                out_ref[m, row : row + channels] = mean
    for m in range(copies):
        out_ref[m, HALO * width :] = message_ref[...]


def mean_call(place, own, near, beside, over, message, copies):
    depth = own.shape[1]
    width = depth - 2 * SPAN
    rows = HALO * width + message.shape[0]
    return pl.pallas_call(
        mean_body,
        out_shape=jax.ShapeDtypeStruct((copies, rows, LANES), BF16),
        in_specs=[smem()] + [vmem()] * 5,
        out_specs=vmem(),
        scratch_shapes=[pltpu.VMEM((HALO, depth, LANES), F32)],
        cost_estimate=pl.CostEstimate(
            flops=1_000_000, bytes_accessed=600_000, transcendentals=0
        ),
        compiler_params=pltpu.CompilerParams(vmem_limit_bytes=ROOM),
        name="mean",
    )(place, own, near, beside, over, message)


def update_body(
    fill_ref,
    place_ref,
    mean_ref,
    atoms_ref,
    left_ref,
    right_ref,
    gate_ref,
    hidden_ref,
    bonds_ref,
    ends_ref,
    bond_out_ref,
    atom_out_ref,
    table_left,
    table_right,
    kept,
):
    quarters = mean_ref.shape[0]
    channels = gate_ref.shape[0] // quarters
    feat = place_ref[0]
    near = [(feat - q + quarters) % quarters for q in range(quarters)]
    after = HALO * SPAN * channels
    features = atoms_ref.shape[1]
    window = HALO * SPAN * LANES
    inputs = quarters * features
    tile = 2 * LANES
    states = jnp.concatenate(
        [atoms_ref[near[f], :, window : window + inputs] for f in range(quarters)], axis=0
    )
    sides = jnp.concatenate([left_ref[...], right_ref[...]], axis=1)
    width = left_ref.shape[1]
    own_start = window // HALO
    for c in range(window // tile):
        columns = slice(c * tile, (c + 1) * tile)
        mean = jnp.concatenate(
            [
                jnp.concatenate(
                    [
                        mean_ref[f, (2 * c + e) * channels : (2 * c + e + 1) * channels]
                        for f in range(quarters)
                    ],
                    axis=0,
                )
                for e in range(2)
            ],
            axis=1,
        )
        mean_in = jnp.concatenate(
            [
                dot(
                    atoms_ref[near[f], :, window + inputs : window + inputs + features],
                    mean,
                    LEFT_FIRST,
                ).astype(BF16)
                for f in range(quarters)
            ],
            axis=0,
        )
        pre = dot(states, mean_in, LEFT_FIRST)
        state = jnp.concatenate([atoms_ref[near[f], :, columns] for f in range(quarters)], axis=0)
        updated = (state.astype(F32) + jax.nn.silu(pre)).astype(BF16)
        place = c * tile - own_start
        if 0 <= place < own_start:
            kept[:, place : place + tile] = updated
        table = dot(updated, sides, LEFT_FIRST).astype(BF16)
        table_left[:, c * width : (c + 1) * width] = table[:, :width]
        table_right[:, c * width : (c + 1) * width] = table[:, width:]
    own = pl.multiple_of(feat * features, features)
    atom_out_ref[...] = kept[pl.ds(own, features), :]
    bonds = bonds_ref.shape[0]
    per_quarter = bonds // quarters
    lane = lax.broadcasted_iota(jnp.int32, (tile, tile), 1)
    row = lax.broadcasted_iota(jnp.int32, (BLOCK, width), 0)
    for t in range(bonds // tile):
        rows = slice(t * tile, (t + 1) * tile)
        mixed = None
        for side, table in ((0, table_left), (1, table_right)):
            end = ends_ref[rows, side : side + 1]
            chosen = jnp.where(end % tile == lane, 1.0, 0.0).astype(BF16)
            found = jnp.dot(chosen, table[...], preferred_element_type=F32)
            high = jnp.broadcast_to(end // tile, (tile, width))
            for c in range(window // tile):
                part = jnp.where(high == c, found[:, c * width : (c + 1) * width], 0.0)
                mixed = part if mixed is None else mixed + part
        message = jnp.concatenate(
            [
                jnp.concatenate(
                    [
                        mean_ref[f, after + b * channels : after + (b + 1) * channels]
                        for f in range(quarters)
                    ],
                    axis=0,
                )
                for b in range(t * (tile // BLOCK), (t + 1) * (tile // BLOCK))
            ],
            axis=1,
        )
        gate = dot(message, gate_ref[...], LEFT_FIRST)
        q = t * tile // per_quarter
        start = t * tile - q * per_quarter
        hidden = hidden_ref[near[q], start : start + tile].astype(F32)
        update = jax.nn.sigmoid(gate) * (hidden + jax.nn.silu(mixed))
        for e in range(tile // BLOCK):
            part = slice(e * BLOCK, (e + 1) * BLOCK)
            real = row < fill_ref[t * (tile // BLOCK) + e]
            here = slice(t * tile + e * BLOCK, t * tile + (e + 1) * BLOCK)
            bond_out_ref[here] = (
                bonds_ref[here].astype(F32) + jnp.where(real, update[part], 0.0)
            ).astype(BF16)


def update_call(fill, place, mean, atoms, left, right, gate, hidden, bonds, ends):
    features = atoms.shape[1]
    window = HALO * SPAN * LANES
    width = left.shape[1]
    tile = 2 * LANES
    return pl.pallas_call(
        update_body,
        out_shape=(
            jax.ShapeDtypeStruct(bonds.shape, BF16),
            jax.ShapeDtypeStruct((features, window // HALO), BF16),
        ),
        in_specs=[smem(), smem()] + [vmem()] * 8,
        out_specs=(vmem(), vmem()),
        scratch_shapes=[
            pltpu.VMEM((tile, window // tile * width), BF16),
            pltpu.VMEM((tile, window // tile * width), BF16),
            pltpu.VMEM((mean.shape[0] * features, window // HALO), BF16),
        ],
        cost_estimate=pl.CostEstimate(
            flops=2_500_000_000, bytes_accessed=4_000_000, transcendentals=2_000_000
        ),
        compiler_params=pltpu.CompilerParams(vmem_limit_bytes=ROOM),
        name="update",
    )(fill, place, mean, atoms, left, right, gate, hidden, bonds, ends)


def local(
    bond_state,
    block_fill,
    w_in,
    w_down,
    pair_coef,
    pair_source,
    pair_owner,
    pair_target,
    w_gate,
    w_atom_in,
    atom_state,
    w_atom,
    bond_ends,
    w_left,
    w_right,
):
    spaces = lax.axis_size("space")
    feats = lax.axis_size("feat")
    space = lax.axis_index("space").astype(jnp.int32).reshape(1)
    feat = lax.axis_index("feat").astype(jnp.int32).reshape(1)
    bonds, _ = bond_state.shape
    blocks = block_fill.shape[0]
    pairs = pair_source.shape[0]
    channels = w_down.shape[1] // feats
    own_bonds = bonds // feats
    near_groups = [[4 * i + k for k in range(4)] for i in range(spaces // 4)]
    first_of = [4 * i for i in range(spaces // 4)]
    next_pairs = swapped(first_of, spaces, 1)
    over_pairs = swapped([i + k for i in first_of for k in (0, 1)], spaces, 2)
    half = channels // 2
    stride = SLOTS * half + 1

    lower = lax.ppermute(atom_state, "space", [(i, (i + 1) % spaces) for i in range(spaces)])
    upper = lax.ppermute(atom_state, "space", [((i + 1) % spaces, i) for i in range(spaces)])
    entered = entry_call(bond_state, w_in, w_down.T, feats)
    entered = exchanged(entered, "feat")
    owners = pair_owner[:, 0]
    before = lax.broadcasted_iota(jnp.int32, (pairs, pairs), 1) < lax.broadcasted_iota(
        jnp.int32, (pairs, pairs), 0
    )
    same = before & (owners[:, None] == owners[None, :])
    rank = jnp.sum(jnp.where(same, 1, 0), axis=1)
    slots = owners * stride + rank * half
    flat = owners * SLOTS + rank
    wanted = flat[:, None] == lax.broadcasted_iota(jnp.int32, (pairs, spaces * SLOTS), 1)
    labels = blocks + jnp.sum(jnp.where(wanted, pair_target[:, None] - blocks, 0), axis=0)
    lane = lax.broadcasted_iota(jnp.int32, (spaces, SLOTS, LANES), 2)
    labels = jnp.where(lane == space[0], labels.reshape(spaces, SLOTS, 1), 0).astype(BF16)
    ends = bond_ends.T
    entered, ends, slots, labels = lax.optimization_barrier((entered, ends, slots, labels))
    hidden, angular = angular_call(block_fill, feat, entered, own_bonds, blocks // feats, channels)
    angular = exchanged(angular, "feat")
    angular, lower, upper = lax.optimization_barrier((angular, lower, upper))
    angular = angular.reshape(blocks, *angular.shape[2:])
    outgoing = contribution_call(pair_source, slots, labels, angular, pair_coef)
    outgoing, hidden = lax.optimization_barrier((outgoing, hidden))
    arrived = exchanged(outgoing.reshape(spaces, stride, *outgoing.shape[1:]), "space")
    arrived = arrived.reshape(outgoing.shape)
    atoms = jnp.concatenate([lower, atom_state, upper, w_atom, w_atom_in], axis=1)
    turned = [hidden[k] if k == 0 else moved(hidden[k], "feat", k) for k in range(feats)]
    hidden = jnp.stack(turned)
    atoms = jnp.stack(
        [atoms if k == 0 else moved(atoms, "feat", k) for k in range(feats)]
    )
    arrived, hidden, atoms = lax.optimization_barrier((arrived, hidden, atoms))
    message, own, near, beside, over = message_call(block_fill, space, bond_ends, arrived, channels)
    near = exchanged(near, "space", near_groups)
    beside = lax.ppermute(beside, "space", next_pairs)
    over = lax.ppermute(over, "space", over_pairs)
    mean = mean_call(space, own, near, beside, over, message, feats)
    mean = exchanged(mean, "feat")
    return update_call(
        block_fill, feat, mean, atoms, w_left, w_right, w_gate, hidden, bond_state, ends
    )


def solution(mesh):
    placed = (
        P("space", "feat"),
        P("space"),
        P(None, "feat"),
        P("feat", None),
        P("space", None, None),
        P("space"),
        P("space", None),
        P("space"),
        P(None, "feat"),
        P(None, "feat"),
        P("feat", "space"),
        P("feat", None),
        P(None, "space"),
        P(None, "feat"),
        P(None, "feat"),
    )
    return jax.shard_map(
        local,
        mesh=mesh,
        in_specs=placed,
        out_specs=(P("space", "feat"), P("feat", "space")),
        check_vma=False,
    )
```

```python
import functools

import jax
import jax.numpy as jnp
from jax import lax
from jax.experimental import pallas as pl
from jax.experimental.pallas import tpu as pltpu
from jax.sharding import PartitionSpec as P


BF16 = jnp.bfloat16
F32 = jnp.float32
BLOCK = 128
LANES = 128
SLOTS = 2
SPAN = 4
HALO = 3
ROOM = 24 << 20
WIDE = 58 << 20
LEFT_FIRST = (((0,), (0,)), ((), ()))
BOTH_LAST = (((1,), (1,)), ((), ()))


def vmem():
    return pl.BlockSpec(memory_space=pltpu.VMEM)


def smem():
    return pl.BlockSpec(memory_space=pltpu.SMEM)


def dot(a, b, dims):
    return lax.dot_general(a, b, dims, preferred_element_type=F32)


def exchanged(value, axis, groups=None):
    return lax.all_to_all(
        value, axis, split_axis=0, concat_axis=0, tiled=True, axis_index_groups=groups
    )


def moved(value, axis, steps):
    count = lax.axis_size(axis)
    return lax.ppermute(value, axis, [(i, (i + steps) % count) for i in range(count)])


def swapped(places, count, step):
    out = []
    for place in places:
        below = (place - step) % count
        out += [(place, below), (below, place)]
    return out


def entry_body(x_hbm, w_hbm, down_ref, out_hbm, x_ref, w_ref, load_sems, store_sems):
    quarters, rows = x_ref.shape[:2]
    inputs = w_ref.shape[0]
    loads = [pltpu.make_async_copy(w_hbm, w_ref, load_sems.at[quarters])]
    for q in range(quarters):
        here = x_hbm.at[pl.ds(q * rows, rows)]
        loads.append(pltpu.make_async_copy(here, x_ref.at[q], load_sems.at[q]))
    for load in loads:
        load.start()
    stores = []

    def store(source, q, first, kind):
        there = out_hbm.at[q, pl.ds(first, source.shape[0])]
        stores.append(pltpu.make_async_copy(source, there, store_sems.at[3 * q + kind]))
        stores[-1].start()

    for q in range(quarters):
        store(down_ref, q, rows + inputs, 0)
    loads[0].wait()
    for q in range(quarters):
        store(w_ref, q, rows, 1)
    for q in range(quarters):
        loads[1 + q].wait()
        store(x_ref.at[q], q, 0, 2)
    for copy in stores:
        copy.wait()


def entry_call(x, w, down, quarters):
    bonds, width = x.shape
    rows = bonds // quarters
    return pl.pallas_call(
        entry_body,
        out_shape=jax.ShapeDtypeStruct((quarters, rows + w.shape[0] + down.shape[0], width), BF16),
        in_specs=[
            pl.BlockSpec(memory_space=pl.ANY),
            pl.BlockSpec(memory_space=pl.ANY),
            vmem(),
        ],
        out_specs=pl.BlockSpec(memory_space=pl.ANY),
        scratch_shapes=[
            pltpu.VMEM((quarters, rows, width), BF16),
            pltpu.VMEM(w.shape, BF16),
            pltpu.SemaphoreType.DMA((quarters + 1,)),
            pltpu.SemaphoreType.DMA((3 * quarters,)),
        ],
        cost_estimate=pl.CostEstimate(flops=0, bytes_accessed=2_000_000, transcendentals=0),
        compiler_params=pltpu.CompilerParams(vmem_limit_bytes=WIDE),
        name="entry",
    )(x, w, down)


def angular_body(fill_ref, place_ref, pack_ref, hidden_ref, angular_ref):
    quarters, own_blocks, channels = angular_ref.shape[:3]
    bonds, width = hidden_ref.shape[1:]
    inputs = quarters * width
    feat = place_ref[0]
    first = feat * own_blocks
    x = jnp.concatenate([pack_ref[k, :bonds] for k in range(quarters)], axis=1)
    total = None
    for q in range(quarters):
        pre = jnp.dot(x, pack_ref[q, bonds : bonds + inputs], preferred_element_type=F32)
        hidden = jax.nn.silu(pre).astype(BF16)
        hidden_ref[(q - feat + quarters) % quarters] = hidden
        part = dot(pack_ref[q, bonds + inputs :], hidden, BOTH_LAST)
        total = part if total is None else total + part
    for b in range(own_blocks):
        piece = total[:, b * BLOCK : (b + 1) * BLOCK]
        real = lax.broadcasted_iota(jnp.int32, piece.shape, 1) < fill_ref[first + b]
        piece = jnp.where(real, piece, 0.0).astype(BF16)
        for q in range(quarters):
            angular_ref[q, b] = piece[q * channels : (q + 1) * channels]


def angular_call(fill, place, pack, bonds, own_blocks, channels):
    quarters, _, width = pack.shape
    return pl.pallas_call(
        angular_body,
        out_shape=(
            jax.ShapeDtypeStruct((quarters, bonds, width), BF16),
            jax.ShapeDtypeStruct((quarters, own_blocks, channels, BLOCK), BF16),
        ),
        in_specs=[smem(), smem(), vmem()],
        out_specs=(vmem(), vmem()),
        cost_estimate=pl.CostEstimate(
            flops=600_000_000, bytes_accessed=2_000_000, transcendentals=262_144
        ),
        compiler_params=pltpu.CompilerParams(vmem_limit_bytes=ROOM),
        name="angular",
    )(fill, place, pack)


def contribution_body(
    chunks, group, source_ref, slot_ref, label_ref, angular_ref, coef_hbm, out_ref, coef_ref, sems
):
    channels, rows = angular_ref.shape[1:]
    half = channels // 2
    stride = SLOTS * half + 1
    per_chunk = coef_ref.shape[0] // chunks
    copies = []
    for c in range(chunks):
        here = pl.ds(c * per_chunk, per_chunk)
        copies.append(pltpu.make_async_copy(coef_hbm.at[here], coef_ref.at[here], sems.at[c]))
        copies[c].start()
    out_ref[...] = jnp.zeros_like(out_ref)

    def tag(step, carry):
        for k in range(4):
            owner = step * 4 + k
            out_ref[owner * stride + stride - 1] = label_ref[owner]
        return carry

    lax.fori_loop(0, label_ref.shape[0] // 4, tag, 0)
    blank = jnp.zeros((channels, rows), BF16)
    for c in range(chunks):
        copies[c].wait()
        for first in range(c * per_chunk, (c + 1) * per_chunk, group):
            pairs = range(first, first + group)
            left = []
            right = []
            for k, pair in enumerate(pairs):
                value = angular_ref[source_ref[pair]]
                sides = [value, blank] if k % 2 == 0 else [blank, value]
                left.append(jnp.concatenate(sides, axis=1))
            for k in range(0, group, 2):
                sides = [coef_ref[first + k], coef_ref[first + k + 1]]
                right.append(jnp.concatenate(sides, axis=1))
            found = dot(jnp.concatenate(left, axis=0), jnp.concatenate(right, axis=0), BOTH_LAST)
            for k, pair in enumerate(pairs):
                column = k // 2 * rows
                part = found[k * channels : (k + 1) * channels, column : column + rows]
                part = part.astype(BF16).reshape(half, 2, rows)
                out_ref[pl.ds(slot_ref[pair], half)] = part


def contribution_call(sources, slots, labels, angular, coef):
    pairs = coef.shape[0]
    chunks, group = next(
        (c, g) for g in (4, 2) for c in (4, 2, 1) if pairs % (c * g) == 0
    )
    _, channels, rows = angular.shape
    stride = SLOTS * channels // 2 + 1
    return pl.pallas_call(
        functools.partial(contribution_body, chunks, group),
        out_shape=jax.ShapeDtypeStruct((labels.shape[0] * stride, 2, rows), BF16),
        in_specs=[
            smem(),
            smem(),
            vmem(),
            vmem(),
            pl.BlockSpec(memory_space=pltpu.HBM),
        ],
        out_specs=vmem(),
        scratch_shapes=[
            pltpu.VMEM(coef.shape, BF16),
            pltpu.SemaphoreType.DMA((chunks,)),
        ],
        cost_estimate=pl.CostEstimate(
            flops=60_000_000, bytes_accessed=5_000_000, transcendentals=0
        ),
        compiler_params=pltpu.CompilerParams(vmem_limit_bytes=WIDE),
        name="contribution",
    )(sources, slots, labels, angular, coef)


def message_body(
    fill_ref,
    place_ref,
    ends_ref,
    arrived_ref,
    message_ref,
    own_ref,
    near_ref,
    next_ref,
    over_ref,
    sums,
    padded,
    chosen,
    labels,
    label_ref,
    sem,
):
    blocks = fill_ref.shape[0]
    channels, rows = sums.shape[1:]
    half = channels // 2
    stride = SLOTS * half + 1
    sources = arrived_ref.shape[0] // stride
    bonds = blocks * rows
    spans = HALO * SPAN
    total = jnp.zeros((2, rows), F32)
    for source in range(sources):
        total += arrived_ref[source * stride + stride - 1].astype(F32)
    labels[...] = total.astype(jnp.int32)
    copy = pltpu.make_async_copy(labels, label_ref, sem)
    copy.start()
    sums[...] = jnp.zeros_like(sums)
    ends = ends_ref[1:2, :]
    high = ends // LANES
    low = ends % LANES
    chosen[...] = jnp.where(
        low == lax.broadcasted_iota(jnp.int32, (LANES, bonds), 0), 1.0, 0.0
    ).astype(BF16)
    copy.wait()

    def add(step, carry):
        for k in range(4):
            source = step * 4 + k
            for slot in range(SLOTS):
                part = arrived_ref[pl.ds(source * stride + slot * half, half)]
                sums[label_ref[slot, source]] += part.reshape(channels, rows).astype(F32)
        return carry

    lax.fori_loop(0, sources // 4, add, 0)
    pieces = []
    masks = []
    for b in range(blocks):
        real = lax.broadcasted_iota(jnp.int32, (channels, rows), 1) < fill_ref[b]
        piece = jnp.where(real, sums[b], 0.0)
        message_ref[b * channels : (b + 1) * channels] = piece.astype(BF16)
        pieces.append(piece)
        masks.append(jnp.where(real[:1], 1.0, 0.0))
    message = jnp.concatenate(pieces, axis=1)
    mask = jnp.concatenate(masks, axis=1)
    stacked = []
    tallies = []
    for h in range(spans):
        here = high == h
        stacked.append(jnp.where(here, message, 0.0).astype(BF16))
        tallies.append(jnp.where(here, mask, 0.0))
    tallies.append(jnp.zeros((16 - spans, bonds), F32))
    stacked.append(jnp.concatenate(tallies, axis=0).astype(BF16))
    window = dot(jnp.concatenate(stacked, axis=0), chosen[...], BOTH_LAST)
    counts = window[spans * channels : spans * channels + spans]
    upper = jnp.floor(counts * (1.0 / 256.0))
    lower = counts - 256.0 * upper
    padded[...] = jnp.zeros_like(padded)
    width = SPAN * channels
    for k in range(HALO):
        group = jnp.concatenate(
            [
                window[k * width : (k + 1) * width],
                upper[k * SPAN : (k + 1) * SPAN],
                lower[k * SPAN : (k + 1) * SPAN],
            ],
            axis=0,
        )
        own_ref[k] = group
        padded[HALO + k] = group.astype(BF16)
    near = place_ref[0] % 4
    for m in range(4):
        start = jnp.where(m == near, 0, m - near + HALO)
        for k in range(HALO):
            near_ref[m, k] = padded[start + k]
    first = HALO + jnp.where(near == 3, 1, 0)
    next_ref[0] = padded[first]
    next_ref[1] = padded[first + 1]
    over_ref[...] = padded[HALO + jnp.where(near >= 2, 2, 0)]


def message_call(fill, place, ends, arrived, channels):
    rows = arrived.shape[2]
    blocks = fill.shape[0]
    depth = SPAN * channels + 2 * SPAN
    return pl.pallas_call(
        message_body,
        out_shape=(
            jax.ShapeDtypeStruct((blocks * channels, rows), BF16),
            jax.ShapeDtypeStruct((HALO, depth, LANES), F32),
            jax.ShapeDtypeStruct((4, HALO, depth, LANES), BF16),
            jax.ShapeDtypeStruct((2, depth, LANES), BF16),
            jax.ShapeDtypeStruct((depth, LANES), BF16),
        ),
        in_specs=[smem(), smem(), vmem(), vmem()],
        out_specs=(vmem(), vmem(), vmem(), vmem(), vmem()),
        scratch_shapes=[
            pltpu.VMEM((blocks + 1, channels, rows), F32),
            pltpu.VMEM((3 * HALO, depth, LANES), BF16),
            pltpu.VMEM((LANES, blocks * rows), BF16),
            pltpu.VMEM((SLOTS, LANES), jnp.int32),
            pltpu.SMEM((SLOTS, LANES), jnp.int32),
            pltpu.SemaphoreType.DMA(()),
        ],
        cost_estimate=pl.CostEstimate(
            flops=120_000_000, bytes_accessed=2_000_000, transcendentals=0
        ),
        compiler_params=pltpu.CompilerParams(vmem_limit_bytes=ROOM),
        name="message",
    )(fill, place, ends, arrived)


def mean_body(place_ref, own_ref, near_ref, next_ref, over_ref, out_ref, total):
    copies = out_ref.shape[0]
    depth = own_ref.shape[1]
    channels = (depth - 2 * SPAN) // SPAN
    width = SPAN * channels
    spot = place_ref[0] % 4
    for k in range(HALO):
        value = own_ref[k]
        for m in range(4):
            value += near_ref[m, k].astype(F32)
        total[k] = value
    first = jnp.where(spot == 3, 1, 0)
    total[first] += next_ref[0].astype(F32)
    total[first + 1] += next_ref[1].astype(F32)
    total[jnp.where(spot >= 2, 2, 0)] += over_ref[...].astype(F32)
    for k in range(HALO):
        value = total[k]
        for h in range(SPAN):
            count = 256.0 * value[width + h : width + h + 1]
            count += value[width + SPAN + h : width + SPAN + h + 1]
            mean = value[h * channels : (h + 1) * channels] / jnp.maximum(count, 1.0)
            mean = mean.astype(BF16)
            row = (k * SPAN + h) * channels
            for m in range(copies):
                out_ref[m, row : row + channels] = mean


def mean_call(place, own, near, beside, over, copies):
    depth = own.shape[1]
    width = depth - 2 * SPAN
    return pl.pallas_call(
        mean_body,
        out_shape=jax.ShapeDtypeStruct((copies, HALO * width, LANES), BF16),
        in_specs=[smem()] + [vmem()] * 4,
        out_specs=vmem(),
        scratch_shapes=[pltpu.VMEM((HALO, depth, LANES), F32)],
        cost_estimate=pl.CostEstimate(
            flops=1_000_000, bytes_accessed=600_000, transcendentals=0
        ),
        compiler_params=pltpu.CompilerParams(vmem_limit_bytes=ROOM),
        name="mean",
    )(place, own, near, beside, over)


def update_body(
    fill_ref,
    place_ref,
    mean_ref,
    atoms_ref,
    left_ref,
    right_ref,
    gate_ref,
    hidden_ref,
    bonds_ref,
    ends_ref,
    *refs,
):
    quarters = mean_ref.shape[0]
    pieces = refs[:quarters]
    bond_out_ref, atom_out_ref, table_left, table_right, kept, message_ref = refs[quarters:]
    channels = gate_ref.shape[0] // quarters
    feat = place_ref[0]
    near = [(feat - q + quarters) % quarters for q in range(quarters)]
    features = atoms_ref.shape[1]
    window = HALO * SPAN * LANES
    inputs = quarters * features
    tile = 2 * LANES
    states = jnp.concatenate(
        [atoms_ref[near[f], :, window : window + inputs] for f in range(quarters)], axis=0
    )
    sides = jnp.concatenate([left_ref[...], right_ref[...]], axis=1)
    width = left_ref.shape[1]
    own_start = window // HALO
    for c in range(window // tile):
        columns = slice(c * tile, (c + 1) * tile)
        mean = jnp.concatenate(
            [
                jnp.concatenate(
                    [
                        mean_ref[f, (2 * c + e) * channels : (2 * c + e + 1) * channels]
                        for f in range(quarters)
                    ],
                    axis=0,
                )
                for e in range(2)
            ],
            axis=1,
        )
        mean_in = jnp.concatenate(
            [
                dot(
                    atoms_ref[near[f], :, window + inputs : window + inputs + features],
                    mean,
                    LEFT_FIRST,
                ).astype(BF16)
                for f in range(quarters)
            ],
            axis=0,
        )
        pre = dot(states, mean_in, LEFT_FIRST)
        state = jnp.concatenate([atoms_ref[near[f], :, columns] for f in range(quarters)], axis=0)
        updated = (state.astype(F32) + jax.nn.silu(pre)).astype(BF16)
        place = c * tile - own_start
        if 0 <= place < own_start:
            kept[:, place : place + tile] = updated
        table = dot(updated, sides, LEFT_FIRST).astype(BF16)
        table_left[:, c * width : (c + 1) * width] = table[:, :width]
        table_right[:, c * width : (c + 1) * width] = table[:, width:]
    own = pl.multiple_of(feat * features, features)
    atom_out_ref[...] = kept[pl.ds(own, features), :]
    for k in range(quarters):
        message_ref[near[k]] = pieces[k][...]
    bonds = bonds_ref.shape[0]
    per_quarter = bonds // quarters
    lane = lax.broadcasted_iota(jnp.int32, (tile, tile), 1)
    row = lax.broadcasted_iota(jnp.int32, (BLOCK, width), 0)
    for t in range(bonds // tile):
        rows = slice(t * tile, (t + 1) * tile)
        mixed = None
        for side, table in ((0, table_left), (1, table_right)):
            end = ends_ref[rows, side : side + 1]
            chosen = jnp.where(end % tile == lane, 1.0, 0.0).astype(BF16)
            found = jnp.dot(chosen, table[...], preferred_element_type=F32)
            high = jnp.broadcast_to(end // tile, (tile, width))
            for c in range(window // tile):
                part = jnp.where(high == c, found[:, c * width : (c + 1) * width], 0.0)
                mixed = part if mixed is None else mixed + part
        message = jnp.concatenate(
            [
                jnp.concatenate(
                    [
                        message_ref[f, b * channels : (b + 1) * channels]
                        for f in range(quarters)
                    ],
                    axis=0,
                )
                for b in range(t * (tile // BLOCK), (t + 1) * (tile // BLOCK))
            ],
            axis=1,
        )
        gate = dot(message, gate_ref[...], LEFT_FIRST)
        q = t * tile // per_quarter
        start = t * tile - q * per_quarter
        hidden = hidden_ref[near[q], start : start + tile].astype(F32)
        update = jax.nn.sigmoid(gate) * (hidden + jax.nn.silu(mixed))
        for e in range(tile // BLOCK):
            part = slice(e * BLOCK, (e + 1) * BLOCK)
            real = row < fill_ref[t * (tile // BLOCK) + e]
            here = slice(t * tile + e * BLOCK, t * tile + (e + 1) * BLOCK)
            bond_out_ref[here] = (
                bonds_ref[here].astype(F32) + jnp.where(real, update[part], 0.0)
            ).astype(BF16)


def update_call(fill, place, mean, atoms, left, right, gate, hidden, bonds, ends, messages):
    features = atoms.shape[1]
    window = HALO * SPAN * LANES
    width = left.shape[1]
    tile = 2 * LANES
    return pl.pallas_call(
        update_body,
        out_shape=(
            jax.ShapeDtypeStruct(bonds.shape, BF16),
            jax.ShapeDtypeStruct((features, window // HALO), BF16),
        ),
        in_specs=[smem(), smem()] + [vmem()] * (8 + len(messages)),
        out_specs=(vmem(), vmem()),
        scratch_shapes=[
            pltpu.VMEM((tile, window // tile * width), BF16),
            pltpu.VMEM((tile, window // tile * width), BF16),
            pltpu.VMEM((mean.shape[0] * features, window // HALO), BF16),
            pltpu.VMEM((len(messages), *messages[0].shape), BF16),
        ],
        cost_estimate=pl.CostEstimate(
            flops=2_500_000_000, bytes_accessed=4_000_000, transcendentals=2_000_000
        ),
        compiler_params=pltpu.CompilerParams(vmem_limit_bytes=ROOM),
        name="update",
    )(fill, place, mean, atoms, left, right, gate, hidden, bonds, ends, *messages)


def local(
    bond_state,
    block_fill,
    w_in,
    w_down,
    pair_coef,
    pair_source,
    pair_owner,
    pair_target,
    w_gate,
    w_atom_in,
    atom_state,
    w_atom,
    bond_ends,
    w_left,
    w_right,
):
    spaces = lax.axis_size("space")
    feats = lax.axis_size("feat")
    space = lax.axis_index("space").astype(jnp.int32).reshape(1)
    feat = lax.axis_index("feat").astype(jnp.int32).reshape(1)
    bonds, _ = bond_state.shape
    blocks = block_fill.shape[0]
    pairs = pair_source.shape[0]
    channels = w_down.shape[1] // feats
    own_bonds = bonds // feats
    near_groups = [[4 * i + k for k in range(4)] for i in range(spaces // 4)]
    first_of = [4 * i for i in range(spaces // 4)]
    next_pairs = swapped(first_of, spaces, 1)
    over_pairs = swapped([i + k for i in first_of for k in (0, 1)], spaces, 2)
    half = channels // 2
    stride = SLOTS * half + 1

    lower = lax.ppermute(atom_state, "space", [(i, (i + 1) % spaces) for i in range(spaces)])
    upper = lax.ppermute(atom_state, "space", [((i + 1) % spaces, i) for i in range(spaces)])
    entered = entry_call(bond_state, w_in, w_down.T, feats)
    entered = exchanged(entered, "feat")
    owners = pair_owner[:, 0]
    before = lax.broadcasted_iota(jnp.int32, (pairs, pairs), 1) < lax.broadcasted_iota(
        jnp.int32, (pairs, pairs), 0
    )
    same = before & (owners[:, None] == owners[None, :])
    rank = jnp.sum(jnp.where(same, 1, 0), axis=1)
    slots = owners * stride + rank * half
    flat = owners * SLOTS + rank
    wanted = flat[:, None] == lax.broadcasted_iota(jnp.int32, (pairs, spaces * SLOTS), 1)
    labels = blocks + jnp.sum(jnp.where(wanted, pair_target[:, None] - blocks, 0), axis=0)
    lane = lax.broadcasted_iota(jnp.int32, (spaces, SLOTS, LANES), 2)
    labels = jnp.where(lane == space[0], labels.reshape(spaces, SLOTS, 1), 0).astype(BF16)
    ends = bond_ends.T
    entered, ends, slots, labels = lax.optimization_barrier((entered, ends, slots, labels))
    hidden, angular = angular_call(block_fill, feat, entered, own_bonds, blocks // feats, channels)
    angular = exchanged(angular, "feat")
    angular, lower, upper = lax.optimization_barrier((angular, lower, upper))
    angular = angular.reshape(blocks, *angular.shape[2:])
    outgoing = contribution_call(pair_source, slots, labels, angular, pair_coef)
    outgoing, hidden = lax.optimization_barrier((outgoing, hidden))
    arrived = exchanged(outgoing.reshape(spaces, stride, *outgoing.shape[1:]), "space")
    arrived = arrived.reshape(outgoing.shape)
    atoms = jnp.concatenate([lower, atom_state, upper, w_atom, w_atom_in], axis=1)
    turned = [hidden[k] if k == 0 else moved(hidden[k], "feat", k) for k in range(feats)]
    hidden = jnp.stack(turned)
    atoms = jnp.stack(
        [atoms if k == 0 else moved(atoms, "feat", k) for k in range(feats)]
    )
    arrived, hidden, atoms = lax.optimization_barrier((arrived, hidden, atoms))
    message, own, near, beside, over = message_call(block_fill, space, bond_ends, arrived, channels)
    near = exchanged(near, "space", near_groups)
    beside = lax.ppermute(beside, "space", next_pairs)
    over = lax.ppermute(over, "space", over_pairs)
    messages = [message if k == 0 else moved(message, "feat", k) for k in range(feats)]
    mean = mean_call(space, own, near, beside, over, feats)
    mean = exchanged(mean, "feat")
    return update_call(
        block_fill,
        feat,
        mean,
        atoms,
        w_left,
        w_right,
        w_gate,
        hidden,
        bond_state,
        ends,
        messages,
    )


def solution(mesh):
    placed = (
        P("space", "feat"),
        P("space"),
        P(None, "feat"),
        P("feat", None),
        P("space", None, None),
        P("space"),
        P("space", None),
        P("space"),
        P(None, "feat"),
        P(None, "feat"),
        P("feat", "space"),
        P("feat", None),
        P(None, "space"),
        P(None, "feat"),
        P(None, "feat"),
    )
    return jax.shard_map(
        local,
        mesh=mesh,
        in_specs=placed,
        out_specs=(P("space", "feat"), P("feat", "space")),
        check_vma=False,
    )
```
